256 devices in a mesh: chan: 128 (over y, x, z_lo, core), cyl: 2 (over z_hi).
Axes of the slice: x: 4, y: 4, z: 8 (z_hi: 2, z_lo: 4; z = z_hi * 4 + z_lo), core: 2. Of those that a mesh axis runs over, the one named last changes fastest.
Arguments:
- volts: bfloat16 [1024, 4, 2, 64, 512], P('chan', 'cyl'), may hold values from -6 to 6
- gain_exponents: int32 [1024, 4], P('chan', 'cyl'), may hold values from -1 to 1
Outputs:
- intensity: float32 [4, 256, 2, 16384], P('cyl', 'chan')
The draws below stay inside these ranges and needn't reach their ends.
All inputs are finite; a program needn't handle non-finite values.
Results may differ from the reference program's by a relative error of at most 0.0042.
Values may be sent and summed in bfloat16 or wider, within the bound.
No kernel may reach another device: no remote copies, remote signals or barrier semaphores. Data moves between devices by JAX's collectives and lax.ppermute only.
A program may use at most 128 MiB of HBM per device.

```python
import math
import jax
import jax.numpy as jnp
from jax import lax

F = 1024
CYLS = 4
FEEDS = 256
POLS = 2
UP = 16
TIME = 64
FRAMES = 2
SUMS = 2
N_CYL = 2


def touch_ends(array, rng, smallest, high):
    shape = array.shape
    place = [jax.random.randint(jax.random.fold_in(rng, axis), (), 0, shape[axis]) for axis in range(len(shape))]
    array = array.at[tuple(place)].set(smallest)
    longest = shape.index(max(shape))
    place[longest] = (place[longest] + 1) % shape[longest]
    return array.at[tuple(place)].set(high)


def steps_of(own_key, extent, shards, low, largest):
    def one(axis_at, shards_of):
        heights = jax.random.uniform(jax.random.fold_in(jax.random.fold_in(own_key, 6), axis_at), (shards_of,), jnp.float32, low / len(shards), largest / len(shards))
        return jnp.repeat(jnp.exp(heights), extent[axis_at] // shards_of).reshape((-1,) + (1,) * (len(extent) - axis_at - 1))

    gain = one(*shards[0])
    for cut in shards[1:]:
        gain = gain * one(*cut)
    return gain


def centred(rng, shape, deviation, reach, cuts=(), kind=jnp.bfloat16):
    drawn = deviation * jax.random.normal(rng, shape, jnp.float32)
    if cuts:
        drawn = drawn * steps_of(rng, shape, cuts, -0.22, 0.18)
    return jnp.clip(drawn, -reach, reach).astype(kind)


def setup_inputs(seed: int = 0) -> dict:
    key_list = jax.random.split(jax.random.key(seed), 3)
    return {
        "volts": centred(key_list[0], (F, CYLS, POLS, TIME, 2 * FEEDS), 1.0, 6.0, ((0, 128), (1, 2))),
        "gain_exponents": touch_ends(jax.random.randint(key_list[1], (F, CYLS), -1, 2), jax.random.fold_in(key_list[1], 1), -1, 1).astype(jnp.int32),
    }


def ns_table(feeds):
    index = jnp.arange(feeds, dtype=jnp.int32)
    product = index[:, None] * (index[None, :] - feeds // 2) % feeds
    theta = product.astype(jnp.float32) * (2.0 * math.pi / feeds)
    cosine = jnp.cos(theta) / math.sqrt(feeds)
    sine = jnp.sin(theta) / math.sqrt(feeds)
    upper = jnp.stack([cosine, -sine], axis=-1).reshape(feeds, 2 * feeds)
    lower = jnp.stack([sine, cosine], axis=-1).reshape(feeds, 2 * feeds)
    return jnp.concatenate([upper, lower], axis=0).astype(jnp.bfloat16)

def up_table(up):
    index = jnp.arange(up, dtype=jnp.int32)
    product = index[:, None] * index[None, :] % up
    theta = product.astype(jnp.float32) * (2.0 * math.pi / up)
    cosine = jnp.cos(theta) / math.sqrt(up)
    sine = jnp.sin(theta) / math.sqrt(up)
    first = jnp.stack([cosine, -sine], axis=1)
    second = jnp.stack([sine, cosine], axis=1)
    return jnp.stack([first, second], axis=0).astype(jnp.bfloat16)

def ew_weights(beam_index, cyl_index, cyls):
    phase = 2.0 * math.pi * cyl_index[None, :].astype(jnp.float32) * (beam_index[:, None].astype(jnp.float32) - (cyls - 1) / 2.0) / cyls
    return (jnp.cos(phase) / 2.0, -jnp.sin(phase) / 2.0)

def combine(real_part, imag_part, w_real, w_imag):
    high = lax.Precision.HIGHEST
    pr = jnp.einsum('ec,ngcpt->ngept', w_real, real_part, precision=high) - jnp.einsum('ec,ngcpt->ngept', w_imag, imag_part, precision=high)
    pi = jnp.einsum('ec,ngcpt->ngept', w_real, imag_part, precision=high) + jnp.einsum('ec,ngcpt->ngept', w_imag, real_part, precision=high)
    return jnp.stack([pr, pi], axis=1)

def reference(volts, gain_exponents):
    group = 8 if F % 8 == 0 else 1
    table = ns_table(FEEDS).astype(jnp.float32)
    upper_table = up_table(UP).astype(jnp.float32)
    per_group = CYLS // N_CYL
    beam_index = jnp.arange(CYLS, dtype=jnp.int32)

    def one_block(pieces):
        block, exps = pieces
        ns_beams = lax.dot_general(table, block.astype(jnp.float32), (((0,), (4,)), ((), ())), precision=lax.Precision.HIGHEST)
        ns_beams = ns_beams.reshape(FEEDS, 2, group, CYLS, POLS, TIME)
        beams = None
        for part in range(N_CYL):
            cyl_index = part * per_group + jnp.arange(per_group, dtype=jnp.int32)
            w_real, w_imag = ew_weights(beam_index, cyl_index, CYLS)
            lo = part * per_group
            piece = combine(ns_beams[:, 0, :, lo:lo + per_group], ns_beams[:, 1, :, lo:lo + per_group], w_real, w_imag)
            piece = piece.astype(jnp.bfloat16).astype(jnp.float32)
            beams = piece if beams is None else beams + piece
        gains = jnp.exp2(exps.astype(jnp.float32))
        coded = (beams * gains[None, None, :, :, None, None]).astype(jnp.bfloat16)
        blocks = TIME // UP
        shaped = coded.astype(jnp.float32).reshape(FEEDS, 2, group, CYLS, POLS, blocks, UP)
        spectra = jnp.einsum('nrgepbk,rksm->ngepbsm', shaped, upper_table, precision=lax.Precision.HIGHEST)
        power = lax.optimization_barrier(jnp.sum(spectra * spectra, axis=(3, 5)))
        power = power.reshape(FEEDS, group, CYLS, FRAMES, SUMS, UP).sum(axis=4) / (POLS * SUMS)
        return jnp.transpose(power, (2, 0, 3, 1, 4)).reshape(CYLS, FEEDS, FRAMES, group * UP)
    shaped_volts = volts.reshape(F // group, group, CYLS, POLS, TIME, 2 * FEEDS)
    shaped_exps = gain_exponents.reshape(F // group, group, CYLS)
    result = lax.map(one_block, (shaped_volts, shaped_exps))
    result = jnp.transpose(result, (1, 2, 3, 0, 4))
    return result.reshape(CYLS, FEEDS, FRAMES, F * UP)
```

```python
import math

import jax
import jax.numpy as jnp
import ml_dtypes
import numpy as np
from jax import lax
from jax.experimental import pallas as pl
from jax.experimental.pallas import tpu as pltpu
from jax.sharding import PartitionSpec as P

CYLS = 4
UP = 16
FRAMES = 2
POLS = 2
SUMS = 2
FEEDS = 256
LANES = 128


def ns_rows(feeds):
    feed = np.arange(feeds)
    beam = np.arange(feeds).reshape(feeds // 2, 2).T.reshape(-1)
    theta = (feed[None, :] * (beam[:, None] - feeds // 2) % feeds) * (2.0 * math.pi / feeds)
    cosine = np.cos(theta) / math.sqrt(feeds)
    sine = np.sin(theta) / math.sqrt(feeds)
    real = np.concatenate([cosine, sine], axis=1)
    imag = np.concatenate([-sine, cosine], axis=1)
    return np.concatenate([real, imag], axis=0).astype(np.float32).astype(ml_dtypes.bfloat16)


def up_columns(up, chans):
    index = np.arange(up)
    theta = (index[:, None] * index[None, :] % up) * (2.0 * math.pi / up)
    cosine = np.cos(theta) / math.sqrt(up)
    sine = np.sin(theta) / math.sqrt(up)
    eye = np.eye(chans)
    table = [[np.kron(eye, cosine), np.kron(eye, -sine)], [np.kron(eye, sine), np.kron(eye, cosine)]]
    return np.block(table).astype(np.float32).astype(ml_dtypes.bfloat16)


def rounded(value):
    return value.astype(jnp.bfloat16).astype(jnp.float32)


def ew_beams(real, imag):
    s = math.sqrt(0.5) / 2.0
    h0r, h0i = real[0] * 0.5, imag[0] * 0.5
    n1r, n1i = real[1] * s, imag[1] * s
    a1, b1 = n1r + n1i, n1r - n1i
    h2r, h2i = real[2] * 0.5, imag[2] * 0.5
    n3r, n3i = real[3] * s, imag[3] * s
    a3, b3 = n3r + n3i, n3r - n3i
    first = [
        (h0r - a1, h0i + b1),
        (h0r + b1, h0i + a1),
        (h0r + a1, h0i - b1),
        (h0r - b1, h0i - a1),
    ]
    second = [
        (h2i + b3, a3 - h2r),
        (-h2i - a3, h2r + b3),
        (h2i - b3, -h2r - a3),
        (a3 - h2i, h2r - b3),
    ]
    return [
        (
            (rounded(f[0]) + rounded(g[0])).astype(jnp.bfloat16),
            (rounded(f[1]) + rounded(g[1])).astype(jnp.bfloat16),
        )
        for f, g in zip(first, second)
    ]


def step_kernel(first, last, *refs):
    refs = list(refs)
    k_ref, own_ref, recv_ref, t_ref, u_ref = refs[:5]
    refs = refs[5:]
    acc_in = None if first else refs.pop(0)
    scale_ref = refs.pop(0) if last else None
    out_ref = refs.pop(0)
    x_ref = refs.pop(0)
    stage_ref = refs.pop(0) if last else None
    k = k_ref[0]
    for cyl in range(2):
        mine = pl.ds(pl.multiple_of((2 * k + cyl) * LANES, LANES), LANES)
        other = pl.ds(pl.multiple_of((2 * (1 - k) + cyl) * LANES, LANES), LANES)
        x_ref[mine, :] = own_ref[:, cyl, 0].reshape(LANES, 2 * FEEDS)
        x_ref[other, :] = recv_ref[:, cyl].reshape(LANES, 2 * FEEDS)
    dims = (((1,), (1,)), ((), ()))
    half = FEEDS // 2
    for low in range(2):
        x = x_ref[...]
        rows = pl.ds(low * half, half)
        real = lax.dot_general(t_ref[rows, :], x, dims, preferred_element_type=jnp.float32)
        rows_i = pl.ds(FEEDS + low * half, half)
        imag = lax.dot_general(t_ref[rows_i, :], x, dims, preferred_element_type=jnp.float32)
        cut = lambda v: [v[:, c * LANES : (c + 1) * LANES] for c in range(CYLS)]
        coded = ew_beams(cut(real), cut(imag))
        for e in range(CYLS):
            both = jnp.concatenate(coded[e], axis=1)
            spectra = jnp.dot(both, u_ref[...], preferred_element_type=jnp.float32)
            squared = spectra * spectra
            power = squared[:, :LANES] + squared[:, LANES:]
            if not first:
                power = acc_in[e, rows, :] + power
            if last:
                stage_ref[pl.ds(2 * e + low, half, stride=8), :] = power * scale_ref[pl.ds(e, 1), :]
            else:
                out_ref[e, rows, :] = power
    if last:
        out_ref[...] = stage_ref[...].astype(jnp.bfloat16)


def step(pol, block, first, last, k, volts, recv, table, up_table, acc, scale):
    chans, cyls = volts.shape[:2]
    whole = lambda a: pl.BlockSpec(a.shape, lambda i, kk: (0,) * a.ndim)
    args = [volts, recv, table, up_table]
    specs = [
        pl.BlockSpec(
            (chans, cyls, 1, UP, 2 * FEEDS), lambda i, kk: (0, 0, pol, SUMS * kk[0] + block, 0)
        ),
        whole(recv),
        whole(table),
        whole(up_table),
    ]
    aliases = {}
    if not first:
        aliases = {} if last else {len(args) + 1: 0}
        args.append(acc)
        specs.append(whole(acc))
    if last:
        args.append(scale)
        specs.append(whole(scale))
        out = jax.ShapeDtypeStruct((FEEDS * CYLS, LANES), jnp.bfloat16)
    else:
        out = jax.ShapeDtypeStruct((CYLS, FEEDS, LANES), jnp.float32)
    scratch = [pltpu.VMEM((CYLS * LANES, 2 * FEEDS), jnp.bfloat16)]
    if last:
        scratch.append(pltpu.VMEM((FEEDS * CYLS, LANES), jnp.float32))
    flops = 2 * 512 * 512 * 512 + 2 * CYLS * 256 * 256 * 256
    return pl.pallas_call(
        lambda *refs: step_kernel(first, last, *refs),
        out_shape=out,
        grid_spec=pltpu.PrefetchScalarGridSpec(
            num_scalar_prefetch=1,
            grid=(1,),
            in_specs=specs,
            out_specs=whole(out),
            scratch_shapes=scratch,
        ),
        input_output_aliases=aliases,
        cost_estimate=pl.CostEstimate(flops=flops, bytes_accessed=2 << 20, transcendentals=0),
        compiler_params=pltpu.CompilerParams(vmem_limit_bytes=24 << 20),
        name="beam_step_last" if last else "beam_step",
    )(k, *args)


def place_kernel(in_ref, out_ref, wide_ref):
    wide_ref[...] = in_ref[...].astype(jnp.float32)
    for row in range(4):
        out_ref[row] = wide_ref[pl.ds(row, 256, stride=4), :]


def place(arrived):
    return pl.pallas_call(
        place_kernel,
        out_shape=jax.ShapeDtypeStruct((4, 256, LANES), jnp.float32),
        scratch_shapes=[pltpu.VMEM((1024, LANES), jnp.float32)],
        compiler_params=pltpu.CompilerParams(vmem_limit_bytes=24 << 20),
        name="place",
    )(arrived)


def local(volts, gain_exponents):
    chans, cyls = volts.shape[:2]
    k = lax.axis_index("cyl")
    pair = [(0, 1), (1, 0)]
    table = jnp.asarray(ns_rows(FEEDS))
    up_table = jnp.asarray(up_columns(UP, chans))
    steps = [(pol, block) for pol in range(POLS) for block in range(SUMS)]
    received = []
    source = volts
    for pol, block in steps:
        start = (1 - k) * (SUMS * UP) + block * UP
        piece = lax.dynamic_slice(source, (0, 0, pol, start, 0), (chans, cyls, 1, UP, 2 * FEEDS))
        source, piece = lax.optimization_barrier((source, piece))
        received.append(lax.ppermute(piece.reshape(chans, cyls, UP, 2 * FEEDS), "cyl", pair))
    others = lax.ppermute(gain_exponents, "cyl", pair)
    low = jnp.where(k == 0, gain_exponents, others)
    high = jnp.where(k == 0, others, gain_exponents)
    gains = jnp.exp2(2.0 * jnp.concatenate([low, high], axis=1).astype(jnp.float32)) / (POLS * SUMS)
    scale = jnp.repeat(gains.T, UP, axis=1)
    which = k.astype(jnp.int32).reshape(1)
    acc = None
    for index, (pol, block) in enumerate(steps):
        first, last = index == 0, index == len(steps) - 1
        acc = step(pol, block, first, last, which, volts, received[index], table, up_table, acc, scale)
    sent = acc.reshape(256, 4, LANES)
    arrived = lax.all_to_all(sent, ("chan", "cyl"), split_axis=0, concat_axis=0, tiled=True)
    placed = place(arrived.reshape(1024, LANES))
    placed = placed.reshape(2, 2, 128, FRAMES, LANES).transpose(0, 1, 3, 2, 4)
    return placed.reshape(2, 2, FRAMES, 128 * LANES)


def solution(mesh):
    return jax.shard_map(
        local,
        mesh=mesh,
        in_specs=(P("chan", "cyl", None, None, None), P("chan", "cyl")),
        out_specs=P("cyl", "chan", None, None),
        check_vma=False,
    )
```

```python
import math

import jax
import jax.numpy as jnp
import ml_dtypes
import numpy as np
from jax import lax
from jax.experimental import pallas as pl
from jax.experimental.pallas import tpu as pltpu
from jax.sharding import PartitionSpec as P

CYLS = 4
UP = 16
FRAMES = 2
POLS = 2
SUMS = 2
FEEDS = 256
LANES = 128


def ns_rows(feeds):
    feed = np.arange(feeds)
    beam = np.arange(feeds).reshape(feeds // 2, 2).T.reshape(-1)
    theta = (feed[None, :] * (beam[:, None] - feeds // 2) % feeds) * (2.0 * math.pi / feeds)
    cosine = np.cos(theta) / math.sqrt(feeds)
    sine = np.sin(theta) / math.sqrt(feeds)
    real = np.concatenate([cosine, sine], axis=1)
    imag = np.concatenate([-sine, cosine], axis=1)
    return np.concatenate([real, imag], axis=0).astype(np.float32).astype(ml_dtypes.bfloat16)


def up_columns(up, chans):
    index = np.arange(up)
    theta = (index[:, None] * index[None, :] % up) * (2.0 * math.pi / up)
    cosine = np.cos(theta) / math.sqrt(up)
    sine = np.sin(theta) / math.sqrt(up)
    eye = np.eye(chans)
    table = [[np.kron(eye, cosine), np.kron(eye, -sine)], [np.kron(eye, sine), np.kron(eye, cosine)]]
    return np.block(table).astype(np.float32).astype(ml_dtypes.bfloat16)


def rounded(value):
    return value.astype(jnp.bfloat16).astype(jnp.float32)


def ew_beams(real, imag):
    s = math.sqrt(0.5) / 2.0
    h0r, h0i = real[0] * 0.5, imag[0] * 0.5
    n1r, n1i = real[1] * s, imag[1] * s
    a1, b1 = n1r + n1i, n1r - n1i
    h2r, h2i = real[2] * 0.5, imag[2] * 0.5
    n3r, n3i = real[3] * s, imag[3] * s
    a3, b3 = n3r + n3i, n3r - n3i
    first = [
        (h0r - a1, h0i + b1),
        (h0r + b1, h0i + a1),
        (h0r + a1, h0i - b1),
        (h0r - b1, h0i - a1),
    ]
    second = [
        (h2i + b3, a3 - h2r),
        (-h2i - a3, h2r + b3),
        (h2i - b3, -h2r - a3),
        (a3 - h2i, h2r - b3),
    ]
    return [
        (
            (rounded(f[0]) + rounded(g[0])).astype(jnp.bfloat16),
            (rounded(f[1]) + rounded(g[1])).astype(jnp.bfloat16),
        )
        for f, g in zip(first, second)
    ]


def gain_rows(k, own_ref, other_ref):
    own = own_ref[...].astype(jnp.float32)
    other = other_ref[...].astype(jnp.float32)
    chans = own.shape[0]
    lane = lax.broadcasted_iota(jnp.int32, (chans, LANES), 1)
    chan = lax.broadcasted_iota(jnp.int32, (chans, LANES), 0)
    hit = lane // UP == chan
    rows = []
    for pair in (jnp.where(k == 0, own, other), jnp.where(k == 0, other, own)):
        for beam in range(2):
            gain = jnp.broadcast_to(pair[:, beam : beam + 1], (chans, LANES))
            row = jnp.sum(jnp.where(hit, gain, 0.0), axis=0, keepdims=True)
            rows.append(jnp.exp2(2.0 * row) / (POLS * SUMS))
    return rows


def step_kernel(first, last, *refs):
    refs = list(refs)
    k_ref, own_ref, recv_ref, t_ref, u_ref = refs[:5]
    refs = refs[5:]
    acc_in = None if first else refs.pop(0)
    gain_refs = [refs.pop(0), refs.pop(0)] if last else None
    out_ref = refs.pop(0)
    x_ref = refs.pop(0)
    stage_ref = refs.pop(0) if last else None
    k = k_ref[0]
    for cyl in range(2):
        mine = pl.ds(pl.multiple_of((2 * k + cyl) * LANES, LANES), LANES)
        other = pl.ds(pl.multiple_of((2 * (1 - k) + cyl) * LANES, LANES), LANES)
        x_ref[mine, :] = own_ref[:, cyl, 0].reshape(LANES, 2 * FEEDS)
        x_ref[other, :] = recv_ref[:, cyl].reshape(LANES, 2 * FEEDS)
    if last:
        scale = gain_rows(k, *gain_refs)
    dims = (((1,), (1,)), ((), ()))
    half = FEEDS // 2
    for low in range(2):
        x = x_ref[...]
        rows = pl.ds(low * half, half)
        real = lax.dot_general(t_ref[rows, :], x, dims, preferred_element_type=jnp.float32)
        rows_i = pl.ds(FEEDS + low * half, half)
        imag = lax.dot_general(t_ref[rows_i, :], x, dims, preferred_element_type=jnp.float32)
        cut = lambda v: [v[:, c * LANES : (c + 1) * LANES] for c in range(CYLS)]
        coded = ew_beams(cut(real), cut(imag))
        for e in range(CYLS):
            both = jnp.concatenate(coded[e], axis=1)
            spectra = jnp.dot(both, u_ref[...], preferred_element_type=jnp.float32)
            squared = spectra * spectra
            power = squared[:, :LANES] + squared[:, LANES:]
            if not first:
                power = acc_in[e, rows, :] + power
            if last:
                stage_ref[pl.ds(2 * e + low, half, stride=8), :] = power * scale[e]
            else:
                out_ref[e, rows, :] = power
    if last:
        out_ref[...] = stage_ref[...].astype(jnp.bfloat16)


def step(pol, block, first, last, k, volts, recv, table, up_table, acc, gains):
    chans, cyls = volts.shape[:2]
    whole = lambda a: pl.BlockSpec(a.shape, lambda i, kk: (0,) * a.ndim)
    args = [volts, recv, table, up_table]
    specs = [
        pl.BlockSpec(
            (chans, cyls, 1, UP, 2 * FEEDS), lambda i, kk: (0, 0, pol, SUMS * kk[0] + block, 0)
        ),
        whole(recv),
        whole(table),
        whole(up_table),
    ]
    aliases = {}
    if not first:
        aliases = {} if last else {len(args) + 1: 0}
        args.append(acc)
        specs.append(whole(acc))
    if last:
        args.extend(gains)
        specs.extend(whole(g) for g in gains)
        out = jax.ShapeDtypeStruct((FEEDS * CYLS, LANES), jnp.bfloat16)
    else:
        out = jax.ShapeDtypeStruct((CYLS, FEEDS, LANES), jnp.float32)
    scratch = [pltpu.VMEM((CYLS * LANES, 2 * FEEDS), jnp.bfloat16)]
    if last:
        scratch.append(pltpu.VMEM((FEEDS * CYLS, LANES), jnp.float32))
    flops = 2 * 512 * 512 * 512 + 2 * CYLS * 256 * 256 * 256
    return pl.pallas_call(
        lambda *refs: step_kernel(first, last, *refs),
        out_shape=out,
        grid_spec=pltpu.PrefetchScalarGridSpec(
            num_scalar_prefetch=1,
            grid=(1,),
            in_specs=specs,
            out_specs=whole(out),
            scratch_shapes=scratch,
        ),
        input_output_aliases=aliases,
        cost_estimate=pl.CostEstimate(flops=flops, bytes_accessed=2 << 20, transcendentals=0),
        compiler_params=pltpu.CompilerParams(vmem_limit_bytes=8 << 20),
        name="beam_step_last" if last else "beam_step",
    )(k, *args)


def split_kernel(steps, k_ref, volts_ref, *refs):
    outs, sems = refs[:-1], refs[-1]
    start = (1 - k_ref[0]) * (SUMS * UP)
    copies = []
    for index, (pol, block) in enumerate(steps):
        rows = pl.ds(pl.multiple_of(start + block * UP, UP), UP)
        copies.append(pltpu.make_async_copy(volts_ref.at[:, :, pol, rows, :], outs[index], sems.at[index]))
    for copy in copies:
        copy.start()
    for copy in copies:
        copy.wait()


def split(volts, which, steps):
    chans, cyls = volts.shape[:2]
    piece = jax.ShapeDtypeStruct((chans, cyls, UP, 2 * FEEDS), volts.dtype)
    count = len(steps)
    return pl.pallas_call(
        lambda *refs: split_kernel(steps, *refs),
        out_shape=[piece] * count,
        grid_spec=pltpu.PrefetchScalarGridSpec(
            num_scalar_prefetch=1,
            grid=(1,),
            in_specs=[pl.BlockSpec(memory_space=pltpu.HBM)],
            out_specs=[pl.BlockSpec(memory_space=pltpu.VMEM)] * count,
            scratch_shapes=[pltpu.SemaphoreType.DMA((count,))],
        ),
        compiler_params=pltpu.CompilerParams(vmem_limit_bytes=2 << 20),
        name="split",
    )(which, volts)


def place_kernel(in_ref, out_ref, wide_ref):
    wide_ref[...] = in_ref[...].astype(jnp.float32)
    for row in range(4):
        out_ref[row] = wide_ref[pl.ds(row, 256, stride=4), :]


def place(arrived):
    return pl.pallas_call(
        place_kernel,
        out_shape=jax.ShapeDtypeStruct((4, 256, LANES), jnp.float32),
        scratch_shapes=[pltpu.VMEM((1024, LANES), jnp.float32)],
        compiler_params=pltpu.CompilerParams(vmem_limit_bytes=8 << 20),
        name="place",
    )(arrived)


def local(volts, gain_exponents):
    chans, cyls = volts.shape[:2]
    k = lax.axis_index("cyl")
    pair = [(0, 1), (1, 0)]
    table = jnp.asarray(ns_rows(FEEDS))
    up_table = jnp.asarray(up_columns(UP, chans))
    steps = [(pol, block) for pol in range(POLS) for block in range(SUMS)]
    which = k.astype(jnp.int32).reshape(1)
    source = pltpu.with_memory_space_constraint(volts, pltpu.HBM)
    pieces = split(source, which, steps[:1]) + split(source, which, steps[1:])
    received = [lax.ppermute(piece, "cyl", pair) for piece in pieces]
    others = lax.ppermute(gain_exponents, "cyl", pair)
    acc = None
    for index, (pol, block) in enumerate(steps):
        first, last = index == 0, index == len(steps) - 1
        acc = step(pol, block, first, last, which, volts, received[index], table, up_table, acc, (gain_exponents, others))
    sent = acc.reshape(256, 4, LANES)
    arrived = lax.all_to_all(sent, ("chan", "cyl"), split_axis=0, concat_axis=0, tiled=True)
    placed = place(arrived.reshape(1024, LANES))
    placed = placed.reshape(2, 2, 128, FRAMES, LANES).transpose(0, 1, 3, 2, 4)
    return placed.reshape(2, 2, FRAMES, 128 * LANES)


def solution(mesh):
    return jax.shard_map(
        local,
        mesh=mesh,
        in_specs=(P("chan", "cyl", None, None, None), P("chan", "cyl")),
        out_specs=P("cyl", "chan", None, None),
        check_vma=False,
    )
```

```python
import math

import jax
import jax.numpy as jnp
import ml_dtypes
import numpy as np
from jax import lax
from jax.experimental import pallas as pl
from jax.experimental.pallas import tpu as pltpu
from jax.sharding import PartitionSpec as P

CYLS = 4
UP = 16
FRAMES = 2
POLS = 2
SUMS = 2
FEEDS = 256
LANES = 128


def ns_rows(feeds):
    feed = np.arange(feeds)
    beam = np.arange(feeds).reshape(feeds // 2, 2).T.reshape(-1)
    theta = (feed[None, :] * (beam[:, None] - feeds // 2) % feeds) * (2.0 * math.pi / feeds)
    cosine = np.cos(theta) / math.sqrt(feeds)
    sine = np.sin(theta) / math.sqrt(feeds)
    real = np.concatenate([cosine, sine], axis=1)
    imag = np.concatenate([-sine, cosine], axis=1)
    return np.concatenate([real, imag], axis=0).astype(np.float32).astype(ml_dtypes.bfloat16)


def up_columns(up, chans):
    index = np.arange(up)
    theta = (index[:, None] * index[None, :] % up) * (2.0 * math.pi / up)
    cosine = np.cos(theta) / math.sqrt(up)
    sine = np.sin(theta) / math.sqrt(up)
    eye = np.eye(chans)
    table = [[np.kron(eye, cosine), np.kron(eye, -sine)], [np.kron(eye, sine), np.kron(eye, cosine)]]
    return np.block(table).astype(np.float32).astype(ml_dtypes.bfloat16)


def ew_partials(real, imag, sign):
    half = 0.5 * sign
    diag = math.sqrt(0.5) / 2.0 * sign
    hr, hi = real[0] * half, imag[0] * half
    nr, ni = real[1] * diag, imag[1] * diag
    a, b = nr + ni, nr - ni
    beams = [(hr - a, hi + b), (hr + b, hi + a), (hr + a, hi - b), (hr - b, hi - a)]
    return [(r.astype(jnp.bfloat16), i.astype(jnp.bfloat16)) for r, i in beams]


def ns_partials(x, t_ref, low, sign):
    dims = (((1,), (1,)), ((), ()))
    half = FEEDS // 2
    real = lax.dot_general(t_ref[pl.ds(low * half, half), :], x, dims, preferred_element_type=jnp.float32)
    imag = lax.dot_general(t_ref[pl.ds(FEEDS + low * half, half), :], x, dims, preferred_element_type=jnp.float32)
    cut = lambda v: [v[:, :LANES], v[:, LANES:]]
    return ew_partials(cut(real), cut(imag), sign)


def pair_rows(read):
    return jnp.concatenate([read(cyl).reshape(LANES, 2 * FEEDS) for cyl in range(2)], axis=0)


def gain_rows(k, own_ref, other_ref):
    own = own_ref[...].astype(jnp.float32)
    other = other_ref[...].astype(jnp.float32)
    chans = own.shape[0]
    lane = lax.broadcasted_iota(jnp.int32, (chans, LANES), 1)
    chan = lax.broadcasted_iota(jnp.int32, (chans, LANES), 0)
    hit = lane // UP == chan
    rows = []
    for pair in (jnp.where(k == 0, own, other), jnp.where(k == 0, other, own)):
        for beam in range(2):
            gain = jnp.broadcast_to(pair[:, beam : beam + 1], (chans, LANES))
            row = jnp.sum(jnp.where(hit, gain, 0.0), axis=0, keepdims=True)
            rows.append(jnp.exp2(2.0 * row) / (POLS * SUMS))
    return rows


def own_kernel(k_ref, own_ref, t_ref, out_ref):
    x = pair_rows(lambda cyl: own_ref[:, cyl, 0])
    half = FEEDS // 2
    for low in range(2):
        for e, parts in enumerate(ns_partials(x, t_ref, low, 1.0)):
            for part in range(2):
                out_ref[0, e, part, pl.ds(low * half, half), :] = parts[part]


def own_partials(volts, table, k):
    chans, cyls = volts.shape[:2]
    shape = (POLS * SUMS, CYLS, 2, FEEDS, LANES)
    return pl.pallas_call(
        own_kernel,
        out_shape=jax.ShapeDtypeStruct(shape, jnp.bfloat16),
        grid_spec=pltpu.PrefetchScalarGridSpec(
            num_scalar_prefetch=1,
            grid=(POLS * SUMS,),
            in_specs=[
                pl.BlockSpec(
                    (chans, cyls, 1, UP, 2 * FEEDS),
                    lambda i, kk: (0, 0, i // SUMS, SUMS * kk[0] + i % SUMS, 0),
                ),
                pl.BlockSpec(table.shape, lambda i, kk: (0, 0)),
            ],
            out_specs=pl.BlockSpec((1, *shape[1:]), lambda i, kk: (i, 0, 0, 0, 0)),
        ),
        cost_estimate=pl.CostEstimate(flops=4 * 2 * 512 * 512 * 256, bytes_accessed=4 << 20, transcendentals=0),
        compiler_params=pltpu.CompilerParams(vmem_limit_bytes=8 << 20),
        name="own_partials",
    )(k, volts, table)


def step_kernel(first, last, *refs):
    refs = list(refs)
    k_ref, own_ref, recv_ref, t_ref, u_ref = refs[:5]
    refs = refs[5:]
    acc_in = None if first else refs.pop(0)
    gain_refs = [refs.pop(0), refs.pop(0)] if last else None
    out_ref = refs.pop(0)
    stage_ref = refs.pop(0) if last else None
    k = k_ref[0]
    if last:
        scale = gain_rows(k, *gain_refs)
    sign = (1 - 2 * k).astype(jnp.float32)
    x = pair_rows(lambda cyl: recv_ref[:, cyl])
    half = FEEDS // 2
    for low in range(2):
        rows = pl.ds(low * half, half)
        for e, (other_r, other_i) in enumerate(ns_partials(x, t_ref, low, sign)):
            own_r = own_ref[0, e, 0, rows, :].astype(jnp.float32)
            own_i = own_ref[0, e, 1, rows, :].astype(jnp.float32)
            other_r, other_i = other_r.astype(jnp.float32), other_i.astype(jnp.float32)
            if e % 2 == 0:
                coded = own_r + other_i, own_i - other_r
            else:
                coded = own_r - other_i, own_i + other_r
            both = jnp.concatenate([part.astype(jnp.bfloat16) for part in coded], axis=1)
            spectra = jnp.dot(both, u_ref[...], preferred_element_type=jnp.float32)
            squared = spectra * spectra
            power = squared[:, :LANES] + squared[:, LANES:]
            if not first:
                power = acc_in[e, rows, :] + power
            if last:
                stage_ref[pl.ds(2 * e + low, half, stride=8), :] = power * scale[e]
            else:
                out_ref[e, rows, :] = power
    if last:
        out_ref[...] = stage_ref[...].astype(jnp.bfloat16)


def step(index, first, last, k, own, recv, table, up_table, acc, gains):
    whole = lambda a: pl.BlockSpec(a.shape, lambda i, kk: (0,) * a.ndim)
    args = [own, recv, table, up_table]
    specs = [
        pl.BlockSpec((1, *own.shape[1:]), lambda i, kk: (index, 0, 0, 0, 0)),
        whole(recv),
        whole(table),
        whole(up_table),
    ]
    aliases = {}
    if not first:
        aliases = {} if last else {len(args) + 1: 0}
        args.append(acc)
        specs.append(whole(acc))
    if last:
        args.extend(gains)
        specs.extend(whole(g) for g in gains)
        out = jax.ShapeDtypeStruct((FEEDS * CYLS, LANES), jnp.bfloat16)
    else:
        out = jax.ShapeDtypeStruct((CYLS, FEEDS, LANES), jnp.float32)
    flops = 2 * 512 * 512 * 256 + 2 * CYLS * 256 * 256 * 256
    return pl.pallas_call(
        lambda *refs: step_kernel(first, last, *refs),
        out_shape=out,
        grid_spec=pltpu.PrefetchScalarGridSpec(
            num_scalar_prefetch=1,
            grid=(1,),
            in_specs=specs,
            out_specs=whole(out),
            scratch_shapes=[pltpu.VMEM((FEEDS * CYLS, LANES), jnp.float32)] if last else [],
        ),
        input_output_aliases=aliases,
        cost_estimate=pl.CostEstimate(flops=flops, bytes_accessed=2 << 20, transcendentals=0),
        compiler_params=pltpu.CompilerParams(vmem_limit_bytes=8 << 20),
        name="beam_step_last" if last else "beam_step",
    )(k, *args)


def split_kernel(steps, k_ref, volts_ref, *refs):
    outs, sems = refs[:-1], refs[-1]
    start = (1 - k_ref[0]) * (SUMS * UP)
    copies = []
    for index, (pol, block) in enumerate(steps):
        rows = pl.ds(pl.multiple_of(start + block * UP, UP), UP)
        copies.append(pltpu.make_async_copy(volts_ref.at[:, :, pol, rows, :], outs[index], sems.at[index]))
    for copy in copies:
        copy.start()
    for copy in copies:
        copy.wait()


def split(volts, which, steps):
    chans, cyls = volts.shape[:2]
    piece = jax.ShapeDtypeStruct((chans, cyls, UP, 2 * FEEDS), volts.dtype)
    count = len(steps)
    return pl.pallas_call(
        lambda *refs: split_kernel(steps, *refs),
        out_shape=[piece] * count,
        grid_spec=pltpu.PrefetchScalarGridSpec(
            num_scalar_prefetch=1,
            grid=(1,),
            in_specs=[pl.BlockSpec(memory_space=pltpu.HBM)],
            out_specs=[pl.BlockSpec(memory_space=pltpu.VMEM)] * count,
            scratch_shapes=[pltpu.SemaphoreType.DMA((count,))],
        ),
        compiler_params=pltpu.CompilerParams(vmem_limit_bytes=2 << 20),
        name="split",
    )(which, volts)


def place_kernel(in_ref, out_ref, wide_ref):
    wide_ref[...] = in_ref[...].astype(jnp.float32)
    for row in range(4):
        out_ref[row] = wide_ref[pl.ds(row, 256, stride=4), :]


def place(arrived):
    return pl.pallas_call(
        place_kernel,
        out_shape=jax.ShapeDtypeStruct((4, 256, LANES), jnp.float32),
        scratch_shapes=[pltpu.VMEM((1024, LANES), jnp.float32)],
        compiler_params=pltpu.CompilerParams(vmem_limit_bytes=8 << 20),
        name="place",
    )(arrived)


def local(volts, gain_exponents):
    chans, cyls = volts.shape[:2]
    k = lax.axis_index("cyl")
    pair = [(0, 1), (1, 0)]
    table = jnp.asarray(ns_rows(FEEDS))
    up_table = jnp.asarray(up_columns(UP, chans))
    steps = [(pol, block) for pol in range(POLS) for block in range(SUMS)]
    which = k.astype(jnp.int32).reshape(1)
    source = pltpu.with_memory_space_constraint(volts, pltpu.HBM)
    pieces = split(source, which, steps[:1]) + split(source, which, steps[1:])
    received = [lax.ppermute(piece, "cyl", pair) for piece in pieces]
    others = lax.ppermute(gain_exponents, "cyl", pair)
    own = own_partials(source, table, which)
    acc = None
    gains = (gain_exponents, others)
    for index in range(len(steps)):
        first, last = index == 0, index == len(steps) - 1
        acc = step(index, first, last, which, own, received[index], table, up_table, acc, gains)
    sent = acc.reshape(256, 4, LANES)
    arrived = lax.all_to_all(sent, ("chan", "cyl"), split_axis=0, concat_axis=0, tiled=True)
    placed = place(arrived.reshape(1024, LANES))
    placed = placed.reshape(2, 2, 128, FRAMES, LANES).transpose(0, 1, 3, 2, 4)
    return placed.reshape(2, 2, FRAMES, 128 * LANES)


def solution(mesh):
    return jax.shard_map(
        local,
        mesh=mesh,
        in_specs=(P("chan", "cyl", None, None, None), P("chan", "cyl")),
        out_specs=P("cyl", "chan", None, None),
        check_vma=False,
    )
```

```python
import math

import jax
import jax.numpy as jnp
import ml_dtypes
import numpy as np
from jax import lax
from jax.experimental import pallas as pl
from jax.experimental.pallas import tpu as pltpu
from jax.sharding import PartitionSpec as P

CYLS = 4
UP = 16
FRAMES = 2
POLS = 2
SUMS = 2
FEEDS = 256
LANES = 128


def ns_rows(feeds):
    feed = np.arange(feeds)
    beam = np.arange(feeds).reshape(feeds // 2, 2).T.reshape(-1)
    theta = (feed[None, :] * (beam[:, None] - feeds // 2) % feeds) * (2.0 * math.pi / feeds)
    cosine = np.cos(theta) / math.sqrt(feeds)
    sine = np.sin(theta) / math.sqrt(feeds)
    real = np.concatenate([cosine, sine], axis=1)
    imag = np.concatenate([-sine, cosine], axis=1)
    return np.concatenate([real, imag], axis=0).astype(np.float32).astype(ml_dtypes.bfloat16)


def up_columns(up, chans):
    index = np.arange(up)
    theta = (index[:, None] * index[None, :] % up) * (2.0 * math.pi / up)
    cosine = np.cos(theta) / math.sqrt(up)
    sine = np.sin(theta) / math.sqrt(up)
    eye = np.eye(chans)
    table = [[np.kron(eye, cosine), np.kron(eye, -sine)], [np.kron(eye, sine), np.kron(eye, cosine)]]
    return np.block(table).astype(np.float32).astype(ml_dtypes.bfloat16)


def ew_partials(real, imag, sign):
    half = 0.5 * sign
    diag = math.sqrt(0.5) / 2.0 * sign
    hr, hi = real[0] * half, imag[0] * half
    nr, ni = real[1] * diag, imag[1] * diag
    a, b = nr + ni, nr - ni
    beams = [(hr - a, hi + b), (hr + b, hi + a), (hr + a, hi - b), (hr - b, hi - a)]
    return [(r.astype(jnp.bfloat16), i.astype(jnp.bfloat16)) for r, i in beams]


def ns_partials(x, t_ref, low, sign):
    dims = (((1,), (1,)), ((), ()))
    half = FEEDS // 2
    real = lax.dot_general(t_ref[pl.ds(low * half, half), :], x, dims, preferred_element_type=jnp.float32)
    imag = lax.dot_general(t_ref[pl.ds(FEEDS + low * half, half), :], x, dims, preferred_element_type=jnp.float32)
    cut = lambda v: [v[:, :LANES], v[:, LANES:]]
    return ew_partials(cut(real), cut(imag), sign)


def pair_rows(read):
    return jnp.concatenate([read(cyl).reshape(LANES, 2 * FEEDS) for cyl in range(2)], axis=0)


def gain_rows(k, own_ref, other_ref):
    own = own_ref[...].astype(jnp.float32)
    other = other_ref[...].astype(jnp.float32)
    chans = own.shape[0]
    lane = lax.broadcasted_iota(jnp.int32, (chans, LANES), 1)
    chan = lax.broadcasted_iota(jnp.int32, (chans, LANES), 0)
    hit = lane // UP == chan
    rows = []
    for pair in (jnp.where(k == 0, own, other), jnp.where(k == 0, other, own)):
        for beam in range(2):
            gain = jnp.broadcast_to(pair[:, beam : beam + 1], (chans, LANES))
            row = jnp.sum(jnp.where(hit, gain, 0.0), axis=0, keepdims=True)
            rows.append(jnp.exp2(2.0 * row) / (POLS * SUMS))
    return rows


def own_kernel(k_ref, own_ref, t_ref, out_ref):
    x = pair_rows(lambda cyl: own_ref[:, cyl, 0])
    half = FEEDS // 2
    for low in range(2):
        for e, parts in enumerate(ns_partials(x, t_ref, low, 1.0)):
            for part in range(2):
                out_ref[0, e, part, pl.ds(low * half, half), :] = parts[part]


def own_partials(volts, table, k):
    chans, cyls = volts.shape[:2]
    shape = (POLS * SUMS, CYLS, 2, FEEDS, LANES)
    return pl.pallas_call(
        own_kernel,
        out_shape=jax.ShapeDtypeStruct(shape, jnp.bfloat16),
        grid_spec=pltpu.PrefetchScalarGridSpec(
            num_scalar_prefetch=1,
            grid=(POLS * SUMS,),
            in_specs=[
                pl.BlockSpec(
                    (chans, cyls, 1, UP, 2 * FEEDS),
                    lambda i, kk: (0, 0, i // SUMS, SUMS * kk[0] + i % SUMS, 0),
                ),
                pl.BlockSpec(table.shape, lambda i, kk: (0, 0)),
            ],
            out_specs=pl.BlockSpec((1, *shape[1:]), lambda i, kk: (i, 0, 0, 0, 0)),
        ),
        cost_estimate=pl.CostEstimate(flops=4 * 2 * 512 * 512 * 256, bytes_accessed=4 << 20, transcendentals=0),
        compiler_params=pltpu.CompilerParams(vmem_limit_bytes=8 << 20),
        name="own_partials",
    )(k, volts, table)


def step_kernel(first, last, *refs):
    refs = list(refs)
    k_ref, own_ref, recv_ref, t_ref, u_ref = refs[:5]
    refs = refs[5:]
    acc_in = None if first else refs.pop(0)
    gain_refs = [refs.pop(0), refs.pop(0)] if last else None
    out_ref = refs.pop(0)
    stage_ref = refs.pop(0) if last else None
    k = k_ref[0]
    if last:
        scale = gain_rows(k, *gain_refs)
    sign = (1 - 2 * k).astype(jnp.float32)
    x = pair_rows(lambda cyl: recv_ref[:, cyl])
    half = FEEDS // 2
    for low in range(2):
        rows = pl.ds(low * half, half)
        for e, (other_r, other_i) in enumerate(ns_partials(x, t_ref, low, sign)):
            own_r, own_i = own_ref[0, e, 0, rows, :], own_ref[0, e, 1, rows, :]
            if e % 2 == 0:
                coded = own_r + other_i, own_i - other_r
            else:
                coded = own_r - other_i, own_i + other_r
            both = jnp.concatenate(coded, axis=1)
            spectra = jnp.dot(both, u_ref[...], preferred_element_type=jnp.float32)
            squared = spectra * spectra
            power = squared[:, :LANES] + squared[:, LANES:]
            if not first:
                power = acc_in[e, rows, :] + power
            if last:
                stage_ref[pl.ds(2 * e + low, half, stride=8), :] = power * scale[e]
            else:
                out_ref[e, rows, :] = power
    if last:
        out_ref[...] = stage_ref[...].astype(jnp.bfloat16)


def step(index, first, last, k, own, recv, table, up_table, acc, gains):
    whole = lambda a: pl.BlockSpec(a.shape, lambda i, kk: (0,) * a.ndim)
    args = [own, recv, table, up_table]
    specs = [
        pl.BlockSpec((1, *own.shape[1:]), lambda i, kk: (index, 0, 0, 0, 0)),
        whole(recv),
        whole(table),
        whole(up_table),
    ]
    aliases = {}
    if not first:
        aliases = {} if last else {len(args) + 1: 0}
        args.append(acc)
        specs.append(whole(acc))
    if last:
        args.extend(gains)
        specs.extend(whole(g) for g in gains)
        out = jax.ShapeDtypeStruct((FEEDS * CYLS, LANES), jnp.bfloat16)
    else:
        out = jax.ShapeDtypeStruct((CYLS, FEEDS, LANES), jnp.float32)
    flops = 2 * 512 * 512 * 256 + 2 * CYLS * 256 * 256 * 256
    return pl.pallas_call(
        lambda *refs: step_kernel(first, last, *refs),
        out_shape=out,
        grid_spec=pltpu.PrefetchScalarGridSpec(
            num_scalar_prefetch=1,
            grid=(1,),
            in_specs=specs,
            out_specs=whole(out),
            scratch_shapes=[pltpu.VMEM((FEEDS * CYLS, LANES), jnp.float32)] if last else [],
        ),
        input_output_aliases=aliases,
        cost_estimate=pl.CostEstimate(flops=flops, bytes_accessed=2 << 20, transcendentals=0),
        compiler_params=pltpu.CompilerParams(vmem_limit_bytes=8 << 20),
        name="beam_step_last" if last else "beam_step",
    )(k, *args)


def split_kernel(steps, k_ref, volts_ref, *refs):
    outs, sems = refs[:-1], refs[-1]
    start = (1 - k_ref[0]) * (SUMS * UP)
    copies = []
    for index, (pol, block) in enumerate(steps):
        rows = pl.ds(pl.multiple_of(start + block * UP, UP), UP)
        copies.append(pltpu.make_async_copy(volts_ref.at[:, :, pol, rows, :], outs[index], sems.at[index]))
    for copy in copies:
        copy.start()
    for copy in copies:
        copy.wait()


def split(volts, which, steps):
    chans, cyls = volts.shape[:2]
    piece = jax.ShapeDtypeStruct((chans, cyls, UP, 2 * FEEDS), volts.dtype)
    count = len(steps)
    return pl.pallas_call(
        lambda *refs: split_kernel(steps, *refs),
        out_shape=[piece] * count,
        grid_spec=pltpu.PrefetchScalarGridSpec(
            num_scalar_prefetch=1,
            grid=(1,),
            in_specs=[pl.BlockSpec(memory_space=pltpu.HBM)],
            out_specs=[pl.BlockSpec(memory_space=pltpu.VMEM)] * count,
            scratch_shapes=[pltpu.SemaphoreType.DMA((count,))],
        ),
        compiler_params=pltpu.CompilerParams(vmem_limit_bytes=2 << 20),
        name="split",
    )(which, volts)


def place_kernel(in_ref, out_ref, wide_ref):
    wide_ref[...] = in_ref[...].astype(jnp.float32)
    for row in range(4):
        out_ref[row] = wide_ref[pl.ds(row, 256, stride=4), :]


def place(arrived):
    return pl.pallas_call(
        place_kernel,
        out_shape=jax.ShapeDtypeStruct((4, 256, LANES), jnp.float32),
        scratch_shapes=[pltpu.VMEM((1024, LANES), jnp.float32)],
        compiler_params=pltpu.CompilerParams(vmem_limit_bytes=8 << 20),
        name="place",
    )(arrived)


def local(volts, gain_exponents):
    chans, cyls = volts.shape[:2]
    k = lax.axis_index("cyl")
    pair = [(0, 1), (1, 0)]
    table = jnp.asarray(ns_rows(FEEDS))
    up_table = jnp.asarray(up_columns(UP, chans))
    steps = [(pol, block) for pol in range(POLS) for block in range(SUMS)]
    which = k.astype(jnp.int32).reshape(1)
    source = pltpu.with_memory_space_constraint(volts, pltpu.HBM)
    pieces = split(source, which, steps[:1]) + split(source, which, steps[1:])
    received = [lax.ppermute(piece, "cyl", pair) for piece in pieces]
    others = lax.ppermute(gain_exponents, "cyl", pair)
    own = own_partials(source, table, which)
    acc = None
    gains = (gain_exponents, others)
    for index in range(len(steps)):
        first, last = index == 0, index == len(steps) - 1
        acc = step(index, first, last, which, own, received[index], table, up_table, acc, gains)
    sent = acc.reshape(256, 4, LANES)
    arrived = lax.all_to_all(sent, ("chan", "cyl"), split_axis=0, concat_axis=0, tiled=True)
    placed = place(arrived.reshape(1024, LANES))
    placed = placed.reshape(2, 2, 128, FRAMES, LANES).transpose(0, 1, 3, 2, 4)
    return placed.reshape(2, 2, FRAMES, 128 * LANES)


def solution(mesh):
    return jax.shard_map(
        local,
        mesh=mesh,
        in_specs=(P("chan", "cyl", None, None, None), P("chan", "cyl")),
        out_specs=P("cyl", "chan", None, None),
        check_vma=False,
    )
```

```python
import math

import jax
import jax.numpy as jnp
import ml_dtypes
import numpy as np
from jax import lax
from jax.experimental import pallas as pl
from jax.experimental.pallas import tpu as pltpu
from jax.sharding import PartitionSpec as P

CYLS = 4
UP = 16
FRAMES = 2
POLS = 2
SUMS = 2
FEEDS = 256
LANES = 128


def ns_rows(feeds):
    feed = np.arange(feeds)
    beam = np.arange(feeds).reshape(feeds // 2, 2).T.reshape(-1)
    theta = (feed[None, :] * (beam[:, None] - feeds // 2) % feeds) * (2.0 * math.pi / feeds)
    cosine = np.cos(theta) / math.sqrt(feeds)
    sine = np.sin(theta) / math.sqrt(feeds)
    real = np.concatenate([cosine, sine], axis=1)
    imag = np.concatenate([-sine, cosine], axis=1)
    return np.concatenate([real, imag], axis=0).astype(np.float32).astype(ml_dtypes.bfloat16)


def up_columns(up, chans):
    index = np.arange(up)
    theta = (index[:, None] * index[None, :] % up) * (2.0 * math.pi / up)
    cosine = np.cos(theta) / math.sqrt(up)
    sine = np.sin(theta) / math.sqrt(up)
    eye = np.eye(chans)
    table = [[np.kron(eye, cosine), np.kron(eye, -sine)], [np.kron(eye, sine), np.kron(eye, cosine)]]
    return np.block(table).astype(np.float32).astype(ml_dtypes.bfloat16)


def ew_partials(real, imag, sign):
    half = 0.5 * sign
    diag = math.sqrt(0.5) / 2.0 * sign
    hr, hi = real[0] * half, imag[0] * half
    nr, ni = real[1] * diag, imag[1] * diag
    a, b = nr + ni, nr - ni
    beams = [(hr - a, hi + b), (hr + b, hi + a), (hr + a, hi - b), (hr - b, hi - a)]
    return [(r.astype(jnp.bfloat16), i.astype(jnp.bfloat16)) for r, i in beams]


def ns_partials(x, t_ref, low, sign, turned=False):
    dims = (((1,), (0 if turned else 1,)), ((), ()))
    half = FEEDS // 2
    real = lax.dot_general(t_ref[pl.ds(low * half, half), :], x, dims, preferred_element_type=jnp.float32)
    imag = lax.dot_general(t_ref[pl.ds(FEEDS + low * half, half), :], x, dims, preferred_element_type=jnp.float32)
    cut = lambda v: [v[:, :LANES], v[:, LANES:]]
    return ew_partials(cut(real), cut(imag), sign)


def pair_rows(read):
    return jnp.concatenate([read(cyl).reshape(LANES, 2 * FEEDS) for cyl in range(2)], axis=0)


def gain_rows(k, own_ref, other_ref):
    own = own_ref[...].astype(jnp.float32)
    other = other_ref[...].astype(jnp.float32)
    chans = own.shape[0]
    lane = lax.broadcasted_iota(jnp.int32, (chans, LANES), 1)
    chan = lax.broadcasted_iota(jnp.int32, (chans, LANES), 0)
    hit = lane // UP == chan
    rows = []
    for pair in (jnp.where(k == 0, own, other), jnp.where(k == 0, other, own)):
        for beam in range(2):
            gain = jnp.broadcast_to(pair[:, beam : beam + 1], (chans, LANES))
            row = jnp.sum(jnp.where(hit, gain, 0.0), axis=0, keepdims=True)
            rows.append(jnp.exp2(2.0 * row) / (POLS * SUMS))
    return rows


def own_kernel(k_ref, own_ref, t_ref, out_ref):
    x = pair_rows(lambda cyl: own_ref[:, cyl, 0])
    half = FEEDS // 2
    for low in range(2):
        for e, parts in enumerate(ns_partials(x, t_ref, low, 1.0)):
            for part in range(2):
                out_ref[0, e, part, pl.ds(low * half, half), :] = parts[part]


def own_partials(volts, table, k):
    chans, cyls = volts.shape[:2]
    shape = (POLS * SUMS, CYLS, 2, FEEDS, LANES)
    return pl.pallas_call(
        own_kernel,
        out_shape=jax.ShapeDtypeStruct(shape, jnp.bfloat16),
        grid_spec=pltpu.PrefetchScalarGridSpec(
            num_scalar_prefetch=1,
            grid=(POLS * SUMS,),
            in_specs=[
                pl.BlockSpec(
                    (chans, cyls, 1, UP, 2 * FEEDS),
                    lambda i, kk: (0, 0, i // SUMS, SUMS * kk[0] + i % SUMS, 0),
                ),
                pl.BlockSpec(table.shape, lambda i, kk: (0, 0)),
            ],
            out_specs=pl.BlockSpec((1, *shape[1:]), lambda i, kk: (i, 0, 0, 0, 0)),
        ),
        cost_estimate=pl.CostEstimate(flops=4 * 2 * 512 * 512 * 256, bytes_accessed=4 << 20, transcendentals=0),
        compiler_params=pltpu.CompilerParams(vmem_limit_bytes=8 << 20),
        name="own_partials",
    )(k, volts, table)


def step_kernel(first, last, *refs):
    refs = list(refs)
    k_ref, own_ref, recv_ref, t_ref, u_ref = refs[:5]
    refs = refs[5:]
    acc_in = None if first else refs.pop(0)
    gain_refs = [refs.pop(0), refs.pop(0)] if last else None
    out_ref = refs.pop(0)
    stage_ref = refs.pop(0) if last else None
    k = k_ref[0]
    if last:
        scale = gain_rows(k, *gain_refs)
    sign = (1 - 2 * k).astype(jnp.float32)
    x = recv_ref[...] if last else pair_rows(lambda cyl: recv_ref[:, cyl])
    half = FEEDS // 2
    for low in range(2):
        rows = pl.ds(low * half, half)
        for e, (other_r, other_i) in enumerate(ns_partials(x, t_ref, low, sign, last)):
            own_r, own_i = own_ref[0, e, 0, rows, :], own_ref[0, e, 1, rows, :]
            if e % 2 == 0:
                coded = own_r + other_i, own_i - other_r
            else:
                coded = own_r - other_i, own_i + other_r
            both = jnp.concatenate(coded, axis=1)
            spectra = jnp.dot(both, u_ref[...], preferred_element_type=jnp.float32)
            squared = spectra * spectra
            power = squared[:, :LANES] + squared[:, LANES:]
            if not first:
                power = acc_in[e, rows, :] + power
            if last:
                stage_ref[pl.ds(2 * e + low, half, stride=8), :] = power * scale[e]
            else:
                out_ref[e, rows, :] = power
    if last:
        out_ref[...] = stage_ref[...].astype(jnp.bfloat16)


def step(index, first, last, k, own, recv, table, up_table, acc, gains):
    whole = lambda a: pl.BlockSpec(a.shape, lambda i, kk: (0,) * a.ndim)
    args = [own, recv, table, up_table]
    specs = [
        pl.BlockSpec((1, *own.shape[1:]), lambda i, kk: (index, 0, 0, 0, 0)),
        whole(recv),
        whole(table),
        whole(up_table),
    ]
    aliases = {}
    if not first:
        aliases = {} if last else {len(args) + 1: 0}
        args.append(acc)
        specs.append(whole(acc))
    if last:
        args.extend(gains)
        specs.extend(whole(g) for g in gains)
        out = jax.ShapeDtypeStruct((FEEDS * CYLS, LANES), jnp.bfloat16)
    else:
        out = jax.ShapeDtypeStruct((CYLS, FEEDS, LANES), jnp.float32)
    flops = 2 * 512 * 512 * 256 + 2 * CYLS * 256 * 256 * 256
    return pl.pallas_call(
        lambda *refs: step_kernel(first, last, *refs),
        out_shape=out,
        grid_spec=pltpu.PrefetchScalarGridSpec(
            num_scalar_prefetch=1,
            grid=(1,),
            in_specs=specs,
            out_specs=whole(out),
            scratch_shapes=[pltpu.VMEM((FEEDS * CYLS, LANES), jnp.float32)] if last else [],
        ),
        input_output_aliases=aliases,
        cost_estimate=pl.CostEstimate(flops=flops, bytes_accessed=2 << 20, transcendentals=0),
        compiler_params=pltpu.CompilerParams(vmem_limit_bytes=8 << 20),
        name="beam_step_last" if last else "beam_step",
    )(k, *args)


def split_kernel(steps, k_ref, volts_ref, *refs):
    outs, sems = refs[:-1], refs[-1]
    start = (1 - k_ref[0]) * (SUMS * UP)
    copies = []
    for index, (pol, block) in enumerate(steps):
        rows = pl.ds(pl.multiple_of(start + block * UP, UP), UP)
        copies.append(pltpu.make_async_copy(volts_ref.at[:, :, pol, rows, :], outs[index], sems.at[index]))
    for copy in copies:
        copy.start()
    for copy in copies:
        copy.wait()


def split(volts, which, steps):
    chans, cyls = volts.shape[:2]
    piece = jax.ShapeDtypeStruct((chans, cyls, UP, 2 * FEEDS), volts.dtype)
    count = len(steps)
    return pl.pallas_call(
        lambda *refs: split_kernel(steps, *refs),
        out_shape=[piece] * count,
        grid_spec=pltpu.PrefetchScalarGridSpec(
            num_scalar_prefetch=1,
            grid=(1,),
            in_specs=[pl.BlockSpec(memory_space=pltpu.HBM)],
            out_specs=[pl.BlockSpec(memory_space=pltpu.VMEM)] * count,
            scratch_shapes=[pltpu.SemaphoreType.DMA((count,))],
        ),
        compiler_params=pltpu.CompilerParams(vmem_limit_bytes=2 << 20),
        name="split",
    )(which, volts)


def turn_kernel(k_ref, volts_ref, out_ref):
    out_ref[...] = pair_rows(lambda cyl: volts_ref[:, cyl, 0]).T


def turned_piece(volts, which, pol, block):
    chans, cyls = volts.shape[:2]
    return pl.pallas_call(
        turn_kernel,
        out_shape=jax.ShapeDtypeStruct((2 * FEEDS, 2 * LANES), volts.dtype),
        grid_spec=pltpu.PrefetchScalarGridSpec(
            num_scalar_prefetch=1,
            grid=(1,),
            in_specs=[
                pl.BlockSpec(
                    (chans, cyls, 1, UP, 2 * FEEDS),
                    lambda i, kk: (0, 0, pol, SUMS * (1 - kk[0]) + block, 0),
                )
            ],
            out_specs=pl.BlockSpec((2 * FEEDS, 2 * LANES), lambda i, kk: (0, 0)),
        ),
        compiler_params=pltpu.CompilerParams(vmem_limit_bytes=8 << 20),
        name="turned_piece",
    )(which, volts)


def place_kernel(in_ref, out_ref, wide_ref):
    wide_ref[...] = in_ref[...].astype(jnp.float32)
    for row in range(4):
        out_ref[row] = wide_ref[pl.ds(row, 256, stride=4), :]


def place(arrived):
    return pl.pallas_call(
        place_kernel,
        out_shape=jax.ShapeDtypeStruct((4, 256, LANES), jnp.float32),
        scratch_shapes=[pltpu.VMEM((1024, LANES), jnp.float32)],
        compiler_params=pltpu.CompilerParams(vmem_limit_bytes=8 << 20),
        name="place",
    )(arrived)


def local(volts, gain_exponents):
    chans, cyls = volts.shape[:2]
    k = lax.axis_index("cyl")
    pair = [(0, 1), (1, 0)]
    table = jnp.asarray(ns_rows(FEEDS))
    up_table = jnp.asarray(up_columns(UP, chans))
    steps = [(pol, block) for pol in range(POLS) for block in range(SUMS)]
    which = k.astype(jnp.int32).reshape(1)
    source = pltpu.with_memory_space_constraint(volts, pltpu.HBM)
    pieces = [
        *split(source, which, steps[:1]),
        *split(source, which, steps[1:-1]),
        turned_piece(source, which, *steps[-1]),
    ]
    received = [lax.ppermute(piece, "cyl", pair) for piece in pieces]
    others = lax.ppermute(gain_exponents, "cyl", pair)
    own = own_partials(source, table, which)
    acc = None
    gains = (gain_exponents, others)
    for index in range(len(steps)):
        first, last = index == 0, index == len(steps) - 1
        acc = step(index, first, last, which, own, received[index], table, up_table, acc, gains)
    sent = acc.reshape(256, 4, LANES)
    arrived = lax.all_to_all(sent, ("chan", "cyl"), split_axis=0, concat_axis=0, tiled=True)
    placed = place(arrived.reshape(1024, LANES))
    placed = placed.reshape(2, 2, 128, FRAMES, LANES).transpose(0, 1, 3, 2, 4)
    return placed.reshape(2, 2, FRAMES, 128 * LANES)


def solution(mesh):
    return jax.shard_map(
        local,
        mesh=mesh,
        in_specs=(P("chan", "cyl", None, None, None), P("chan", "cyl")),
        out_specs=P("cyl", "chan", None, None),
        check_vma=False,
    )
```

```python
import math

import jax
import jax.numpy as jnp
import ml_dtypes
import numpy as np
from jax import lax
from jax.experimental import pallas as pl
from jax.experimental.pallas import tpu as pltpu
from jax.sharding import PartitionSpec as P

CYLS = 4
UP = 16
FRAMES = 2
POLS = 2
SUMS = 2
FEEDS = 256
LANES = 128


def ns_rows(feeds):
    feed = np.arange(feeds)
    beam = np.arange(feeds).reshape(feeds // 2, 2).T.reshape(-1)
    theta = (feed[None, :] * (beam[:, None] - feeds // 2) % feeds) * (2.0 * math.pi / feeds)
    cosine = np.cos(theta) / math.sqrt(feeds)
    sine = np.sin(theta) / math.sqrt(feeds)
    real = np.concatenate([cosine, sine], axis=1)
    imag = np.concatenate([-sine, cosine], axis=1)
    return np.concatenate([real, imag], axis=0).astype(np.float32).astype(ml_dtypes.bfloat16)


def up_columns(up, chans):
    index = np.arange(up)
    theta = (index[:, None] * index[None, :] % up) * (2.0 * math.pi / up)
    cosine = np.cos(theta) / math.sqrt(up)
    sine = np.sin(theta) / math.sqrt(up)
    eye = np.eye(chans)
    table = [[np.kron(eye, cosine), np.kron(eye, -sine)], [np.kron(eye, sine), np.kron(eye, cosine)]]
    return np.block(table).astype(np.float32).astype(ml_dtypes.bfloat16)


def ew_partials(real, imag, sign):
    half = 0.5 * sign
    diag = math.sqrt(0.5) / 2.0 * sign
    hr, hi = real[0] * half, imag[0] * half
    nr, ni = real[1] * diag, imag[1] * diag
    a, b = nr + ni, nr - ni
    beams = [(hr - a, hi + b), (hr + b, hi + a), (hr + a, hi - b), (hr - b, hi - a)]
    return [(r.astype(jnp.bfloat16), i.astype(jnp.bfloat16)) for r, i in beams]


def ns_partials(x, t_ref, low, sign, turned=False):
    dims = (((1,), (0 if turned else 1,)), ((), ()))
    half = FEEDS if turned else FEEDS // 2
    real = lax.dot_general(t_ref[pl.ds(low * half, half), :], x, dims, preferred_element_type=jnp.float32)
    imag = lax.dot_general(t_ref[pl.ds(FEEDS + low * half, half), :], x, dims, preferred_element_type=jnp.float32)
    cut = lambda v: [v[:, :LANES], v[:, LANES:]]
    return ew_partials(cut(real), cut(imag), sign)


def pair_rows(read):
    return jnp.concatenate([read(cyl).reshape(LANES, 2 * FEEDS) for cyl in range(2)], axis=0)


def gain_rows(k, own_ref, other_ref):
    own = own_ref[...].astype(jnp.float32)
    other = other_ref[...].astype(jnp.float32)
    chans = own.shape[0]
    lane = lax.broadcasted_iota(jnp.int32, (chans, LANES), 1)
    chan = lax.broadcasted_iota(jnp.int32, (chans, LANES), 0)
    hit = lane // UP == chan
    rows = []
    for pair in (jnp.where(k == 0, own, other), jnp.where(k == 0, other, own)):
        for beam in range(2):
            gain = jnp.broadcast_to(pair[:, beam : beam + 1], (chans, LANES))
            row = jnp.sum(jnp.where(hit, gain, 0.0), axis=0, keepdims=True)
            rows.append(jnp.exp2(2.0 * row) / (POLS * SUMS))
    return rows


def own_kernel(k_ref, own_ref, t_ref, out_ref):
    x = pair_rows(lambda cyl: own_ref[:, cyl, 0])
    half = FEEDS // 2
    for low in range(2):
        for e, parts in enumerate(ns_partials(x, t_ref, low, 1.0)):
            for part in range(2):
                out_ref[0, e, part, pl.ds(low * half, half), :] = parts[part]


def own_partials(volts, table, k):
    chans, cyls = volts.shape[:2]
    shape = (POLS * SUMS, CYLS, 2, FEEDS, LANES)
    return pl.pallas_call(
        own_kernel,
        out_shape=jax.ShapeDtypeStruct(shape, jnp.bfloat16),
        grid_spec=pltpu.PrefetchScalarGridSpec(
            num_scalar_prefetch=1,
            grid=(POLS * SUMS,),
            in_specs=[
                pl.BlockSpec(
                    (chans, cyls, 1, UP, 2 * FEEDS),
                    lambda i, kk: (0, 0, i // SUMS, SUMS * kk[0] + i % SUMS, 0),
                ),
                pl.BlockSpec(table.shape, lambda i, kk: (0, 0)),
            ],
            out_specs=pl.BlockSpec((1, *shape[1:]), lambda i, kk: (i, 0, 0, 0, 0)),
        ),
        cost_estimate=pl.CostEstimate(flops=4 * 2 * 512 * 512 * 256, bytes_accessed=4 << 20, transcendentals=0),
        compiler_params=pltpu.CompilerParams(vmem_limit_bytes=8 << 20),
        name="own_partials",
    )(k, volts, table)


def step_kernel(first, last, *refs):
    refs = list(refs)
    k_ref, own_ref, recv_ref, t_ref, u_ref = refs[:5]
    refs = refs[5:]
    acc_in = None if first else refs.pop(0)
    gain_refs = [refs.pop(0), refs.pop(0)] if last else None
    out_ref = refs.pop(0)
    stage_ref = refs.pop(0) if last else None
    k = k_ref[0]
    if last:
        scale = gain_rows(k, *gain_refs)
    sign = (1 - 2 * k).astype(jnp.float32)
    x = recv_ref[...] if last else pair_rows(lambda cyl: recv_ref[:, cyl])
    half = FEEDS // 2
    for low in range(1 if last else 2):
        rows = slice(None) if last else pl.ds(low * half, half)
        for e, (other_r, other_i) in enumerate(ns_partials(x, t_ref, low, sign, last)):
            own_r, own_i = own_ref[0, e, 0, rows, :], own_ref[0, e, 1, rows, :]
            if e % 2 == 0:
                coded = own_r + other_i, own_i - other_r
            else:
                coded = own_r - other_i, own_i + other_r
            both = jnp.concatenate(coded, axis=1)
            spectra = jnp.dot(both, u_ref[...], preferred_element_type=jnp.float32)
            squared = spectra * spectra
            power = squared[:, :LANES] + squared[:, LANES:]
            if not first:
                power = acc_in[e, rows, :] + power
            if last:
                power = power * scale[e]
                for bit in range(2):
                    stage_ref[pl.ds(2 * e + bit, half, stride=8), :] = power[bit * half : (bit + 1) * half]
            else:
                out_ref[e, rows, :] = power
    if last:
        out_ref[...] = stage_ref[...].astype(jnp.bfloat16)


def step(index, first, last, k, own, recv, table, up_table, acc, gains):
    whole = lambda a: pl.BlockSpec(a.shape, lambda i, kk: (0,) * a.ndim)
    args = [own, recv, table, up_table]
    specs = [
        pl.BlockSpec((1, *own.shape[1:]), lambda i, kk: (index, 0, 0, 0, 0)),
        whole(recv),
        whole(table),
        whole(up_table),
    ]
    aliases = {}
    if not first:
        aliases = {} if last else {len(args) + 1: 0}
        args.append(acc)
        specs.append(whole(acc))
    if last:
        args.extend(gains)
        specs.extend(whole(g) for g in gains)
        out = jax.ShapeDtypeStruct((FEEDS * CYLS, LANES), jnp.bfloat16)
    else:
        out = jax.ShapeDtypeStruct((CYLS, FEEDS, LANES), jnp.float32)
    flops = 2 * 512 * 512 * 256 + 2 * CYLS * 256 * 256 * 256
    return pl.pallas_call(
        lambda *refs: step_kernel(first, last, *refs),
        out_shape=out,
        grid_spec=pltpu.PrefetchScalarGridSpec(
            num_scalar_prefetch=1,
            grid=(1,),
            in_specs=specs,
            out_specs=whole(out),
            scratch_shapes=[pltpu.VMEM((FEEDS * CYLS, LANES), jnp.float32)] if last else [],
        ),
        input_output_aliases=aliases,
        cost_estimate=pl.CostEstimate(flops=flops, bytes_accessed=2 << 20, transcendentals=0),
        compiler_params=pltpu.CompilerParams(vmem_limit_bytes=8 << 20),
        name="beam_step_last" if last else "beam_step",
    )(k, *args)


def split_kernel(steps, k_ref, volts_ref, *refs):
    outs, sems = refs[:-1], refs[-1]
    start = (1 - k_ref[0]) * (SUMS * UP)
    copies = []
    for index, (pol, block) in enumerate(steps):
        rows = pl.ds(pl.multiple_of(start + block * UP, UP), UP)
        copies.append(pltpu.make_async_copy(volts_ref.at[:, :, pol, rows, :], outs[index], sems.at[index]))
    for copy in copies:
        copy.start()
    for copy in copies:
        copy.wait()


def split(volts, which, steps):
    chans, cyls = volts.shape[:2]
    piece = jax.ShapeDtypeStruct((chans, cyls, UP, 2 * FEEDS), volts.dtype)
    count = len(steps)
    return pl.pallas_call(
        lambda *refs: split_kernel(steps, *refs),
        out_shape=[piece] * count,
        grid_spec=pltpu.PrefetchScalarGridSpec(
            num_scalar_prefetch=1,
            grid=(1,),
            in_specs=[pl.BlockSpec(memory_space=pltpu.HBM)],
            out_specs=[pl.BlockSpec(memory_space=pltpu.VMEM)] * count,
            scratch_shapes=[pltpu.SemaphoreType.DMA((count,))],
        ),
        compiler_params=pltpu.CompilerParams(vmem_limit_bytes=2 << 20),
        name="split",
    )(which, volts)


def turn_kernel(k_ref, volts_ref, out_ref):
    out_ref[...] = pair_rows(lambda cyl: volts_ref[:, cyl, 0]).T


def turned_piece(volts, which, pol, block):
    chans, cyls = volts.shape[:2]
    return pl.pallas_call(
        turn_kernel,
        out_shape=jax.ShapeDtypeStruct((2 * FEEDS, 2 * LANES), volts.dtype),
        grid_spec=pltpu.PrefetchScalarGridSpec(
            num_scalar_prefetch=1,
            grid=(1,),
            in_specs=[
                pl.BlockSpec(
                    (chans, cyls, 1, UP, 2 * FEEDS),
                    lambda i, kk: (0, 0, pol, SUMS * (1 - kk[0]) + block, 0),
                )
            ],
            out_specs=pl.BlockSpec((2 * FEEDS, 2 * LANES), lambda i, kk: (0, 0)),
        ),
        compiler_params=pltpu.CompilerParams(vmem_limit_bytes=8 << 20),
        name="turned_piece",
    )(which, volts)


def place_kernel(in_ref, out_ref, wide_ref):
    wide_ref[...] = in_ref[...].astype(jnp.float32)
    for row in range(4):
        out_ref[row] = wide_ref[pl.ds(row, 256, stride=4), :]


def place(arrived):
    return pl.pallas_call(
        place_kernel,
        out_shape=jax.ShapeDtypeStruct((4, 256, LANES), jnp.float32),
        scratch_shapes=[pltpu.VMEM((1024, LANES), jnp.float32)],
        compiler_params=pltpu.CompilerParams(vmem_limit_bytes=8 << 20),
        name="place",
    )(arrived)


def local(volts, gain_exponents):
    chans, cyls = volts.shape[:2]
    k = lax.axis_index("cyl")
    pair = [(0, 1), (1, 0)]
    table = jnp.asarray(ns_rows(FEEDS))
    up_table = jnp.asarray(up_columns(UP, chans))
    steps = [(pol, block) for pol in range(POLS) for block in range(SUMS)]
    which = k.astype(jnp.int32).reshape(1)
    source = pltpu.with_memory_space_constraint(volts, pltpu.HBM)
    pieces = [
        *split(source, which, steps[:1]),
        *split(source, which, steps[1:-1]),
        turned_piece(source, which, *steps[-1]),
    ]
    received = [lax.ppermute(piece, "cyl", pair) for piece in pieces]
    others = lax.ppermute(gain_exponents, "cyl", pair)
    own = own_partials(source, table, which)
    acc = None
    gains = (gain_exponents, others)
    for index in range(len(steps)):
        first, last = index == 0, index == len(steps) - 1
        acc = step(index, first, last, which, own, received[index], table, up_table, acc, gains)
    sent = acc.reshape(256, 4, LANES)
    arrived = lax.all_to_all(sent, ("chan", "cyl"), split_axis=0, concat_axis=0, tiled=True)
    placed = place(arrived.reshape(1024, LANES))
    placed = placed.reshape(2, 2, 128, FRAMES, LANES).transpose(0, 1, 3, 2, 4)
    return placed.reshape(2, 2, FRAMES, 128 * LANES)


def solution(mesh):
    return jax.shard_map(
        local,
        mesh=mesh,
        in_specs=(P("chan", "cyl", None, None, None), P("chan", "cyl")),
        out_specs=P("cyl", "chan", None, None),
        check_vma=False,
    )
```

```python
import math

import jax
import jax.numpy as jnp
import ml_dtypes
import numpy as np
from jax import lax
from jax.experimental import pallas as pl
from jax.experimental.pallas import tpu as pltpu
from jax.sharding import PartitionSpec as P

CYLS = 4
UP = 16
FRAMES = 2
POLS = 2
SUMS = 2
FEEDS = 256
LANES = 128


def ns_rows(feeds):
    feed = np.arange(feeds)
    beam = np.arange(feeds).reshape(feeds // 2, 2).T.reshape(-1)
    theta = (feed[None, :] * (beam[:, None] - feeds // 2) % feeds) * (2.0 * math.pi / feeds)
    cosine = np.cos(theta) / math.sqrt(feeds)
    sine = np.sin(theta) / math.sqrt(feeds)
    real = np.concatenate([cosine, sine], axis=1)
    imag = np.concatenate([-sine, cosine], axis=1)
    return np.concatenate([real, imag], axis=0).astype(np.float32).astype(ml_dtypes.bfloat16)


def up_columns(up, chans):
    index = np.arange(up)
    theta = (index[:, None] * index[None, :] % up) * (2.0 * math.pi / up)
    cosine = np.cos(theta) / math.sqrt(up)
    sine = np.sin(theta) / math.sqrt(up)
    eye = np.eye(chans)
    table = [[np.kron(eye, cosine), np.kron(eye, -sine)], [np.kron(eye, sine), np.kron(eye, cosine)]]
    return np.block(table).astype(np.float32).astype(ml_dtypes.bfloat16)


def ew_partials(real, imag, sign):
    half = 0.5 * sign
    diag = math.sqrt(0.5) / 2.0 * sign
    hr, hi = real[0] * half, imag[0] * half
    nr, ni = real[1] * diag, imag[1] * diag
    a, b = nr + ni, nr - ni
    beams = [(hr - a, hi + b), (hr + b, hi + a), (hr + a, hi - b), (hr - b, hi - a)]
    return [(r.astype(jnp.bfloat16), i.astype(jnp.bfloat16)) for r, i in beams]


def ns_partials(x, t_ref, low, sign, turned=False):
    dims = (((1,), (0 if turned else 1,)), ((), ()))
    half = FEEDS if turned else FEEDS // 2
    real = lax.dot_general(t_ref[pl.ds(low * half, half), :], x, dims, preferred_element_type=jnp.float32)
    imag = lax.dot_general(t_ref[pl.ds(FEEDS + low * half, half), :], x, dims, preferred_element_type=jnp.float32)
    cut = lambda v: [v[:, :LANES], v[:, LANES:]]
    return ew_partials(cut(real), cut(imag), sign)


def pair_rows(read):
    return jnp.concatenate([read(cyl).reshape(LANES, 2 * FEEDS) for cyl in range(2)], axis=0)


def gain_rows(k, own_ref, other_ref):
    own = own_ref[...].astype(jnp.float32)
    other = other_ref[...].astype(jnp.float32)
    chans = own.shape[0]
    lane = lax.broadcasted_iota(jnp.int32, (chans, LANES), 1)
    chan = lax.broadcasted_iota(jnp.int32, (chans, LANES), 0)
    hit = lane // UP == chan
    rows = []
    for pair in (jnp.where(k == 0, own, other), jnp.where(k == 0, other, own)):
        for beam in range(2):
            gain = jnp.broadcast_to(pair[:, beam : beam + 1], (chans, LANES))
            row = jnp.sum(jnp.where(hit, gain, 0.0), axis=0, keepdims=True)
            rows.append(jnp.exp2(2.0 * row) / (POLS * SUMS))
    return rows


def own_kernel(k_ref, own_ref, t_ref, out_ref):
    x = pair_rows(lambda cyl: own_ref[:, cyl, 0])
    half = FEEDS // 2
    for low in range(2):
        for e, parts in enumerate(ns_partials(x, t_ref, low, 1.0)):
            for part in range(2):
                out_ref[0, e, part, pl.ds(low * half, half), :] = parts[part]


def own_partials(volts, table, k):
    chans, cyls = volts.shape[:2]
    shape = (POLS * SUMS, CYLS, 2, FEEDS, LANES)
    return pl.pallas_call(
        own_kernel,
        out_shape=jax.ShapeDtypeStruct(shape, jnp.bfloat16),
        grid_spec=pltpu.PrefetchScalarGridSpec(
            num_scalar_prefetch=1,
            grid=(POLS * SUMS,),
            in_specs=[
                pl.BlockSpec(
                    (chans, cyls, 1, UP, 2 * FEEDS),
                    lambda i, kk: (0, 0, i // SUMS, SUMS * kk[0] + i % SUMS, 0),
                ),
                pl.BlockSpec(table.shape, lambda i, kk: (0, 0)),
            ],
            out_specs=pl.BlockSpec((1, *shape[1:]), lambda i, kk: (i, 0, 0, 0, 0)),
        ),
        cost_estimate=pl.CostEstimate(flops=4 * 2 * 512 * 512 * 256, bytes_accessed=4 << 20, transcendentals=0),
        compiler_params=pltpu.CompilerParams(vmem_limit_bytes=8 << 20),
        name="own_partials",
    )(k, volts, table)


def step_kernel(first, last, *refs):
    refs = list(refs)
    k_ref, own_ref, recv_ref, t_ref, u_ref = refs[:5]
    refs = refs[5:]
    acc_in = None if first else refs.pop(0)
    gain_refs = [refs.pop(0), refs.pop(0)] if last else None
    out_ref = refs.pop(0)
    stage_ref = refs.pop(0) if last else None
    k = k_ref[0]
    if last:
        scale = gain_rows(k, *gain_refs)
    sign = (1 - 2 * k).astype(jnp.float32)
    x = recv_ref[...] if last else pair_rows(lambda cyl: recv_ref[:, cyl])
    half = FEEDS // 2
    for low in range(1 if last else 2):
        rows = slice(None) if last else pl.ds(low * half, half)
        for e, (other_r, other_i) in enumerate(ns_partials(x, t_ref, low, sign, last)):
            own_r, own_i = own_ref[0, e, 0, rows, :], own_ref[0, e, 1, rows, :]
            if e % 2 == 0:
                coded = own_r + other_i, own_i - other_r
            else:
                coded = own_r - other_i, own_i + other_r
            both = jnp.concatenate(coded, axis=1)
            spectra = jnp.dot(both, u_ref[...], preferred_element_type=jnp.float32)
            squared = spectra * spectra
            power = squared[:, :LANES] + squared[:, LANES:]
            if not first:
                power = acc_in[e, rows, :] + power
            if last:
                power = power * scale[e]
                for bit in range(2):
                    stage_ref[pl.ds(2 * e + bit, half, stride=8), :] = power[bit * half : (bit + 1) * half]
            else:
                out_ref[e, rows, :] = power
    if last:
        out_ref[...] = stage_ref[...].astype(jnp.bfloat16)


def step(index, first, last, k, own, recv, table, up_table, acc, gains):
    whole = lambda a: pl.BlockSpec(a.shape, lambda i, kk: (0,) * a.ndim)
    args = [own, recv, table, up_table]
    specs = [
        pl.BlockSpec((1, *own.shape[1:]), lambda i, kk: (index, 0, 0, 0, 0)),
        whole(recv),
        whole(table),
        whole(up_table),
    ]
    aliases = {}
    if not first:
        aliases = {} if last else {len(args) + 1: 0}
        args.append(acc)
        specs.append(whole(acc))
    if last:
        args.extend(gains)
        specs.extend(whole(g) for g in gains)
        out = jax.ShapeDtypeStruct((FEEDS * CYLS, LANES), jnp.bfloat16)
    else:
        out = jax.ShapeDtypeStruct((CYLS, FEEDS, LANES), jnp.float32)
    flops = 2 * 512 * 512 * 256 + 2 * CYLS * 256 * 256 * 256
    return pl.pallas_call(
        lambda *refs: step_kernel(first, last, *refs),
        out_shape=out,
        grid_spec=pltpu.PrefetchScalarGridSpec(
            num_scalar_prefetch=1,
            grid=(1,),
            in_specs=specs,
            out_specs=whole(out),
            scratch_shapes=[pltpu.VMEM((FEEDS * CYLS, LANES), jnp.float32)] if last else [],
        ),
        input_output_aliases=aliases,
        cost_estimate=pl.CostEstimate(flops=flops, bytes_accessed=2 << 20, transcendentals=0),
        compiler_params=pltpu.CompilerParams(vmem_limit_bytes=8 << 20),
        name="beam_step_last" if last else "beam_step",
    )(k, *args)


def split_kernel(steps, k_ref, volts_ref, *refs):
    outs, sems = refs[:-1], refs[-1]
    start = (1 - k_ref[0]) * (SUMS * UP)
    copies = []
    for index, (pol, block) in enumerate(steps):
        rows = pl.ds(pl.multiple_of(start + block * UP, UP), UP)
        copies.append(pltpu.make_async_copy(volts_ref.at[:, :, pol, rows, :], outs[index], sems.at[index]))
    for copy in copies:
        copy.start()
    for copy in copies:
        copy.wait()


def split(volts, which, steps):
    chans, cyls = volts.shape[:2]
    piece = jax.ShapeDtypeStruct((chans, cyls, UP, 2 * FEEDS), volts.dtype)
    count = len(steps)
    return pl.pallas_call(
        lambda *refs: split_kernel(steps, *refs),
        out_shape=[piece] * count,
        grid_spec=pltpu.PrefetchScalarGridSpec(
            num_scalar_prefetch=1,
            grid=(1,),
            in_specs=[pl.BlockSpec(memory_space=pltpu.HBM)],
            out_specs=[pl.BlockSpec(memory_space=pltpu.VMEM)] * count,
            scratch_shapes=[pltpu.SemaphoreType.DMA((count,))],
        ),
        compiler_params=pltpu.CompilerParams(vmem_limit_bytes=2 << 20),
        name="split",
    )(which, volts)


def turn_kernel(k_ref, volts_ref, out_ref):
    out_ref[...] = pair_rows(lambda cyl: volts_ref[:, cyl, 0]).T


def turned_piece(volts, which, pol, block):
    chans, cyls = volts.shape[:2]
    return pl.pallas_call(
        turn_kernel,
        out_shape=jax.ShapeDtypeStruct((2 * FEEDS, 2 * LANES), volts.dtype),
        grid_spec=pltpu.PrefetchScalarGridSpec(
            num_scalar_prefetch=1,
            grid=(1,),
            in_specs=[
                pl.BlockSpec(
                    (chans, cyls, 1, UP, 2 * FEEDS),
                    lambda i, kk: (0, 0, pol, SUMS * (1 - kk[0]) + block, 0),
                )
            ],
            out_specs=pl.BlockSpec((2 * FEEDS, 2 * LANES), lambda i, kk: (0, 0)),
        ),
        compiler_params=pltpu.CompilerParams(vmem_limit_bytes=8 << 20),
        name="turned_piece",
    )(which, volts)


def place_kernel(in_ref, out_ref, wide_ref):
    first = 2 * pl.program_id(0)

    @pl.when(first == 0)
    def _():
        wide_ref[...] = in_ref[...].astype(jnp.float32)

    for row in range(2):
        out_ref[row] = wide_ref[pl.ds(first + row, 256, stride=4), :]


def place(arrived):
    return pl.pallas_call(
        place_kernel,
        out_shape=jax.ShapeDtypeStruct((4, 256, LANES), jnp.float32),
        grid=(2,),
        in_specs=[pl.BlockSpec((1024, LANES), lambda i: (0, 0))],
        out_specs=pl.BlockSpec((2, 256, LANES), lambda i: (i, 0, 0)),
        scratch_shapes=[pltpu.VMEM((1024, LANES), jnp.float32)],
        compiler_params=pltpu.CompilerParams(vmem_limit_bytes=8 << 20),
        name="place",
    )(arrived)


def local(volts, gain_exponents):
    chans, cyls = volts.shape[:2]
    k = lax.axis_index("cyl")
    pair = [(0, 1), (1, 0)]
    table = jnp.asarray(ns_rows(FEEDS))
    up_table = jnp.asarray(up_columns(UP, chans))
    steps = [(pol, block) for pol in range(POLS) for block in range(SUMS)]
    which = k.astype(jnp.int32).reshape(1)
    source = pltpu.with_memory_space_constraint(volts, pltpu.HBM)
    pieces = [
        *split(source, which, steps[:1]),
        *split(source, which, steps[1:-1]),
        turned_piece(source, which, *steps[-1]),
    ]
    received = [lax.ppermute(piece, "cyl", pair) for piece in pieces]
    others = lax.ppermute(gain_exponents, "cyl", pair)
    own = own_partials(source, table, which)
    acc = None
    gains = (gain_exponents, others)
    for index in range(len(steps)):
        first, last = index == 0, index == len(steps) - 1
        acc = step(index, first, last, which, own, received[index], table, up_table, acc, gains)
    sent = acc.reshape(256, 4, LANES)
    arrived = lax.all_to_all(sent, ("chan", "cyl"), split_axis=0, concat_axis=0, tiled=True)
    placed = place(arrived.reshape(1024, LANES))
    placed = placed.reshape(2, 2, 128, FRAMES, LANES).transpose(0, 1, 3, 2, 4)
    return placed.reshape(2, 2, FRAMES, 128 * LANES)


def solution(mesh):
    return jax.shard_map(
        local,
        mesh=mesh,
        in_specs=(P("chan", "cyl", None, None, None), P("chan", "cyl")),
        out_specs=P("cyl", "chan", None, None),
        check_vma=False,
    )
```

```python
import math

import jax
import jax.numpy as jnp
import ml_dtypes
import numpy as np
from jax import lax
from jax.experimental import pallas as pl
from jax.experimental.pallas import tpu as pltpu
from jax.sharding import PartitionSpec as P

CYLS = 4
UP = 16
FRAMES = 2
POLS = 2
SUMS = 2
FEEDS = 256
LANES = 128


def ns_rows(feeds):
    feed = np.arange(feeds)
    beam = np.arange(feeds).reshape(feeds // 2, 2).T.reshape(-1)
    theta = (feed[None, :] * (beam[:, None] - feeds // 2) % feeds) * (2.0 * math.pi / feeds)
    cosine = np.cos(theta) / math.sqrt(feeds)
    sine = np.sin(theta) / math.sqrt(feeds)
    real = np.concatenate([cosine, sine], axis=1)
    imag = np.concatenate([-sine, cosine], axis=1)
    return np.concatenate([real, imag], axis=0).astype(np.float32).astype(ml_dtypes.bfloat16)


def up_columns(up, chans):
    index = np.arange(up)
    theta = (index[:, None] * index[None, :] % up) * (2.0 * math.pi / up)
    cosine = np.cos(theta) / math.sqrt(up)
    sine = np.sin(theta) / math.sqrt(up)
    eye = np.eye(chans)
    table = [[np.kron(eye, cosine), np.kron(eye, -sine)], [np.kron(eye, sine), np.kron(eye, cosine)]]
    return np.block(table).astype(np.float32).astype(ml_dtypes.bfloat16)


def ew_partials(real, imag, sign):
    half = 0.5 * sign
    diag = math.sqrt(0.5) / 2.0 * sign
    hr, hi = real[0] * half, imag[0] * half
    nr, ni = real[1] * diag, imag[1] * diag
    a, b = nr + ni, nr - ni
    beams = [(hr - a, hi + b), (hr + b, hi + a), (hr + a, hi - b), (hr - b, hi - a)]
    return [(r.astype(jnp.bfloat16), i.astype(jnp.bfloat16)) for r, i in beams]


def ns_partials(x, t_ref, low, sign, turned=False):
    dims = (((1,), (0 if turned else 1,)), ((), ()))
    half = FEEDS if turned else FEEDS // 2
    real = lax.dot_general(t_ref[pl.ds(low * half, half), :], x, dims, preferred_element_type=jnp.float32)
    imag = lax.dot_general(t_ref[pl.ds(FEEDS + low * half, half), :], x, dims, preferred_element_type=jnp.float32)
    cut = lambda v: [v[:, :LANES], v[:, LANES:]]
    return ew_partials(cut(real), cut(imag), sign)


def pair_rows(read):
    return jnp.concatenate([read(cyl).reshape(LANES, 2 * FEEDS) for cyl in range(2)], axis=0)


def gain_rows(k, own_ref, other_ref):
    own = own_ref[...].astype(jnp.float32)
    other = other_ref[...].astype(jnp.float32)
    chans = own.shape[0]
    lane = lax.broadcasted_iota(jnp.int32, (chans, LANES), 1)
    chan = lax.broadcasted_iota(jnp.int32, (chans, LANES), 0)
    hit = lane // UP == chan
    rows = []
    for pair in (jnp.where(k == 0, own, other), jnp.where(k == 0, other, own)):
        for beam in range(2):
            gain = jnp.broadcast_to(pair[:, beam : beam + 1], (chans, LANES))
            row = jnp.sum(jnp.where(hit, gain, 0.0), axis=0, keepdims=True)
            rows.append(jnp.exp2(2.0 * row) / (POLS * SUMS))
    return rows


def own_kernel(k_ref, own_ref, t_ref, out_ref):
    x = pair_rows(lambda cyl: own_ref[:, cyl, 0])
    half = FEEDS // 2
    for low in range(2):
        for e, parts in enumerate(ns_partials(x, t_ref, low, 1.0)):
            for part in range(2):
                out_ref[0, e, part, pl.ds(low * half, half), :] = parts[part]


def own_partials(volts, table, k):
    chans, cyls = volts.shape[:2]
    shape = (POLS * SUMS, CYLS, 2, FEEDS, LANES)
    return pl.pallas_call(
        own_kernel,
        out_shape=jax.ShapeDtypeStruct(shape, jnp.bfloat16),
        grid_spec=pltpu.PrefetchScalarGridSpec(
            num_scalar_prefetch=1,
            grid=(POLS * SUMS,),
            in_specs=[
                pl.BlockSpec(
                    (chans, cyls, 1, UP, 2 * FEEDS),
                    lambda i, kk: (0, 0, i // SUMS, SUMS * kk[0] + i % SUMS, 0),
                ),
                pl.BlockSpec(table.shape, lambda i, kk: (0, 0)),
            ],
            out_specs=pl.BlockSpec((1, *shape[1:]), lambda i, kk: (i, 0, 0, 0, 0)),
        ),
        cost_estimate=pl.CostEstimate(flops=4 * 2 * 512 * 512 * 256, bytes_accessed=4 << 20, transcendentals=0),
        compiler_params=pltpu.CompilerParams(vmem_limit_bytes=8 << 20),
        name="own_partials",
    )(k, volts, table)


def step_kernel(first, last, *refs):
    refs = list(refs)
    own_ref, recv_ref, t_ref, u_ref = refs[:4]
    refs = refs[4:]
    acc_in = None if first else refs.pop(0)
    gain_refs = [refs.pop(0), refs.pop(0)] if last else None
    out_ref = refs.pop(0)
    stage_ref = refs.pop(0) if last else None
    k = lax.axis_index("cyl")
    if last:
        scale = gain_rows(k, *gain_refs)
    sign = (1 - 2 * k).astype(jnp.float32)
    x = recv_ref[...] if last else pair_rows(lambda cyl: recv_ref[:, cyl])
    half = FEEDS // 2
    for low in range(1 if last else 2):
        rows = slice(None) if last else pl.ds(low * half, half)
        for e, (other_r, other_i) in enumerate(ns_partials(x, t_ref, low, sign, last)):
            own_r, own_i = own_ref[0, e, 0, rows, :], own_ref[0, e, 1, rows, :]
            if e % 2 == 0:
                coded = own_r + other_i, own_i - other_r
            else:
                coded = own_r - other_i, own_i + other_r
            both = jnp.concatenate(coded, axis=1)
            spectra = jnp.dot(both, u_ref[...], preferred_element_type=jnp.float32)
            squared = spectra * spectra
            power = squared[:, :LANES] + squared[:, LANES:]
            if not first:
                power = acc_in[e, rows, :] + power
            if last:
                power = power * scale[e]
                for bit in range(2):
                    stage_ref[pl.ds(2 * e + bit, half, stride=8), :] = power[bit * half : (bit + 1) * half]
            else:
                out_ref[e, rows, :] = power
    if last:
        out_ref[...] = stage_ref[...].astype(jnp.bfloat16)


def step(index, first, last, own, recv, table, up_table, acc, gains):
    whole = lambda a: pl.BlockSpec(a.shape, lambda i: (0,) * a.ndim)
    args = [own, recv, table, up_table]
    specs = [
        pl.BlockSpec((1, *own.shape[1:]), lambda i: (index, 0, 0, 0, 0)),
        whole(recv),
        whole(table),
        whole(up_table),
    ]
    aliases = {}
    if not first:
        aliases = {} if last else {len(args): 0}
        args.append(acc)
        specs.append(whole(acc))
    if last:
        args.extend(gains)
        specs.extend(whole(g) for g in gains)
        out = jax.ShapeDtypeStruct((FEEDS * CYLS, LANES), jnp.bfloat16)
    else:
        out = jax.ShapeDtypeStruct((CYLS, FEEDS, LANES), jnp.float32)
    flops = 2 * 512 * 512 * 256 + 2 * CYLS * 256 * 256 * 256
    return pl.pallas_call(
        lambda *refs: step_kernel(first, last, *refs),
        out_shape=out,
        grid=(1,),
        in_specs=specs,
        out_specs=whole(out),
        scratch_shapes=[pltpu.VMEM((FEEDS * CYLS, LANES), jnp.float32)] if last else [],
        input_output_aliases=aliases,
        cost_estimate=pl.CostEstimate(flops=flops, bytes_accessed=2 << 20, transcendentals=0),
        compiler_params=pltpu.CompilerParams(vmem_limit_bytes=8 << 20),
        name="beam_step_last" if last else "beam_step",
    )(*args)


def split_kernel(steps, k_ref, volts_ref, *refs):
    outs, sems = refs[:-1], refs[-1]
    start = (1 - k_ref[0]) * (SUMS * UP)
    copies = []
    for index, (pol, block) in enumerate(steps):
        rows = pl.ds(pl.multiple_of(start + block * UP, UP), UP)
        copies.append(pltpu.make_async_copy(volts_ref.at[:, :, pol, rows, :], outs[index], sems.at[index]))
    for copy in copies:
        copy.start()
    for copy in copies:
        copy.wait()


def split(volts, which, steps):
    chans, cyls = volts.shape[:2]
    piece = jax.ShapeDtypeStruct((chans, cyls, UP, 2 * FEEDS), volts.dtype)
    count = len(steps)
    return pl.pallas_call(
        lambda *refs: split_kernel(steps, *refs),
        out_shape=[piece] * count,
        grid_spec=pltpu.PrefetchScalarGridSpec(
            num_scalar_prefetch=1,
            grid=(1,),
            in_specs=[pl.BlockSpec(memory_space=pltpu.HBM)],
            out_specs=[pl.BlockSpec(memory_space=pltpu.VMEM)] * count,
            scratch_shapes=[pltpu.SemaphoreType.DMA((count,))],
        ),
        compiler_params=pltpu.CompilerParams(vmem_limit_bytes=2 << 20),
        name="split",
    )(which, volts)


def turn_kernel(k_ref, volts_ref, out_ref):
    out_ref[...] = pair_rows(lambda cyl: volts_ref[:, cyl, 0]).T


def turned_piece(volts, which, pol, block):
    chans, cyls = volts.shape[:2]
    return pl.pallas_call(
        turn_kernel,
        out_shape=jax.ShapeDtypeStruct((2 * FEEDS, 2 * LANES), volts.dtype),
        grid_spec=pltpu.PrefetchScalarGridSpec(
            num_scalar_prefetch=1,
            grid=(1,),
            in_specs=[
                pl.BlockSpec(
                    (chans, cyls, 1, UP, 2 * FEEDS),
                    lambda i, kk: (0, 0, pol, SUMS * (1 - kk[0]) + block, 0),
                )
            ],
            out_specs=pl.BlockSpec((2 * FEEDS, 2 * LANES), lambda i, kk: (0, 0)),
        ),
        compiler_params=pltpu.CompilerParams(vmem_limit_bytes=8 << 20),
        name="turned_piece",
    )(which, volts)


def place_kernel(in_ref, out_ref, wide_ref):
    wide_ref[...] = in_ref[...].astype(jnp.float32)
    for row in range(4):
        out_ref[row] = wide_ref[pl.ds(row, 256, stride=4), :]


def place(arrived):
    return pl.pallas_call(
        place_kernel,
        out_shape=jax.ShapeDtypeStruct((4, 256, LANES), jnp.float32),
        scratch_shapes=[pltpu.VMEM((1024, LANES), jnp.float32)],
        compiler_params=pltpu.CompilerParams(vmem_limit_bytes=8 << 20),
        name="place",
    )(arrived)


def local(volts, gain_exponents):
    chans, cyls = volts.shape[:2]
    k = lax.axis_index("cyl")
    pair = [(0, 1), (1, 0)]
    table = jnp.asarray(ns_rows(FEEDS))
    up_table = jnp.asarray(up_columns(UP, chans))
    steps = [(pol, block) for pol in range(POLS) for block in range(SUMS)]
    which = k.astype(jnp.int32).reshape(1)
    source = pltpu.with_memory_space_constraint(volts, pltpu.HBM)
    pieces = [
        *split(source, which, steps[:1]),
        *split(source, which, steps[1:-1]),
        turned_piece(source, which, *steps[-1]),
    ]
    received = [lax.ppermute(piece, "cyl", pair) for piece in pieces]
    others = lax.ppermute(gain_exponents, "cyl", pair)
    own = own_partials(source, table, which)
    acc = None
    gains = (gain_exponents, others)
    for index in range(len(steps)):
        first, last = index == 0, index == len(steps) - 1
        acc = step(index, first, last, own, received[index], table, up_table, acc, gains)
    sent = acc.reshape(256, 4, LANES)
    arrived = lax.all_to_all(sent, ("chan", "cyl"), split_axis=0, concat_axis=0, tiled=True)
    placed = place(arrived.reshape(1024, LANES))
    placed = placed.reshape(2, 2, 128, FRAMES, LANES).transpose(0, 1, 3, 2, 4)
    return placed.reshape(2, 2, FRAMES, 128 * LANES)


def solution(mesh):
    return jax.shard_map(
        local,
        mesh=mesh,
        in_specs=(P("chan", "cyl", None, None, None), P("chan", "cyl")),
        out_specs=P("cyl", "chan", None, None),
        check_vma=False,
    )
```
